128 devices in a mesh: row: 8 (over z_hi, y), col: 16 (over z_lo, x, core).
Axes of the slice: x: 4, y: 4, z: 4 (z_hi: 2, z_lo: 2; z = z_hi * 2 + z_lo), core: 2. Of those that a mesh axis runs over, the one named last changes fastest.
Arguments:
- embed: bfloat16 [65536, 128], P(('row', 'col')), may hold values from -6 to 6
- degree: int32 [65536], P(('row', 'col')), may hold values from 1 to 256
- tile_row: int32 [8, 16, 256], P('row', 'col'), may hold values from 0 to 63
- tile_col: int32 [8, 16, 256], P('row', 'col'), may hold values from 0 to 31
- tile_count: int32 [8, 16], P('row', 'col'), may hold values from 64 to 256, as said below
- tile_values: bfloat16 [8, 16, 256, 128, 128], P('row', 'col'), may hold values from 0 to 1
- new_rows: int32 [32768], P(('row', 'col')), may hold values from 0 to 65535, as said below
- new_bucket: int32 [32768], P(('row', 'col')), may hold values from 0 to 15
- bucket_norm: float32 [16], replicated, may hold values from 0.5 to 4
Outputs:
- new_embed: float32 [32768, 128], P(('row', 'col'))
The draws below stay inside these ranges and needn't reach their ends.
Inputs may be any that keep to these rules, and one draw needn't show every extreme that they name: `tile_count`: at least 64 slots live on each device, and some device has all 256 live. `new_rows`: the new nodes of one device lie in that device's row block.
All inputs are finite; a program needn't handle non-finite values.
Results may differ from the reference program's by a relative error of at most 0.0026.
Values may be sent and summed in bfloat16 or wider, within the bound.
A program may use at most 128 MiB of HBM per device.

```python
import math
import jax
import jax.numpy as jnp
from jax import lax

EMB = 128
TILE = 128
HOPS = 3
BUCKETS = 16
ROWS_DEV = 512
TILES_DEV = 256
NEW_DEV = 256
NODES = 65536
NEW = 32768
N_ROW = 8
N_COL = 16


def draw_tile_count(key, part):
    total = N_ROW * N_COL
    counts = jax.random.randint(key, (total,), TILES_DEV // 4, TILES_DEV + 1)
    where_full = jax.random.randint(jax.random.fold_in(key, 7), (), 0, total)
    counts = counts.at[where_full].set(TILES_DEV)
    return counts.reshape(N_ROW, N_COL).astype(jnp.int32)


def draw_new_rows(key, part):
    total = NEW_DEV * N_ROW * N_COL
    position = jnp.arange(total, dtype=jnp.int32)
    block = position // NEW_DEV // N_COL
    inside = jax.random.randint(key, (total,), 0, N_COL * ROWS_DEV)
    return (block * (N_COL * ROWS_DEV) + inside).astype(jnp.int32)


def with_ends(entries, own_key, smallest, high):
    longest = entries.shape.index(max(entries.shape))
    spots = []
    for shift in (0, 1):
        where = [jax.random.randint(jax.random.fold_in(own_key, axis), (), 0, length) for axis, length in enumerate(entries.shape)]
        where[longest] = (where[longest] + shift) % entries.shape[longest]
        spots.append(tuple(where))
    return entries.at[spots[0]].set(smallest).at[spots[1]].set(high)


def block_levels(rng, extent, pieces, low, largest):
    level = 1.0
    for dim, blocks in pieces:
        draws = jax.random.uniform(jax.random.fold_in(jax.random.fold_in(rng, 6), dim), (blocks,), jnp.float32, low / len(pieces), largest / len(pieces))
        level = level * jnp.repeat(jnp.exp(draws), extent[dim] // blocks).reshape((-1,) + (1,) * (len(extent) - 1 - dim))
    return level


def noise(stream_key, extent, deviation, reach, pieces=(), held_as=jnp.bfloat16):
    array = jax.random.normal(stream_key, extent, jnp.float32) * deviation
    if len(pieces) > 0:
        array = block_levels(stream_key, extent, pieces, -0.22, 0.18) * array
    return jnp.clip(array, min=-reach, max=reach).astype(held_as)


def setup_inputs(seed: int = 0) -> dict:
    seeds = jax.random.split(jax.random.key(seed), 10)
    embed = noise(seeds[0], (NODES, EMB), 1.0, 6.0, ((0, 128),))
    degree = with_ends(jax.random.randint(seeds[1], (NODES,), 1, 257), jax.random.fold_in(seeds[1], 1), 1, 256).astype(jnp.int32)
    tile_row = with_ends(jax.random.randint(seeds[2], (N_ROW, N_COL, TILES_DEV), 0, N_COL * ROWS_DEV // TILE), jax.random.fold_in(seeds[2], 1), 0, (N_COL * ROWS_DEV // TILE) - 1).astype(jnp.int32)
    tile_col = with_ends(jax.random.randint(seeds[3], (N_ROW, N_COL, TILES_DEV), 0, N_ROW * ROWS_DEV // TILE), jax.random.fold_in(seeds[3], 1), 0, (N_ROW * ROWS_DEV // TILE) - 1).astype(jnp.int32)
    tile_count = draw_tile_count(jax.random.fold_in(seeds[9], 71), 0)
    tile_values = jnp.clip(1.0 * jax.random.uniform(seeds[5], (N_ROW, N_COL, TILES_DEV, TILE, TILE), jnp.float32) ** block_levels(seeds[5], (N_ROW, N_COL, TILES_DEV, TILE, TILE), ((0, 8), (1, 16)), -0.2, 0.2), 0.0, 1.0).astype(jnp.bfloat16)
    new_rows = draw_new_rows(jax.random.fold_in(seeds[9], 71), 0)
    new_bucket = with_ends(jax.random.randint(seeds[7], (NEW,), 0, BUCKETS), jax.random.fold_in(seeds[7], 1), 0, BUCKETS - 1).astype(jnp.int32)
    bucket_norm = jnp.clip(jnp.exp(jax.random.uniform(seeds[8], (BUCKETS,), jnp.float32, math.log(0.5), math.log(4.0))), 0.5, 4.0)
    return dict(embed=embed, degree=degree, tile_row=tile_row, tile_col=tile_col, tile_count=tile_count, tile_values=tile_values, new_rows=new_rows, new_bucket=new_bucket, bucket_norm=bucket_norm)


def one_hop(state, tile_row, tile_col, tile_count, tile_values):
    grid = state.reshape(N_ROW, N_COL, ROWS_DEV, EMB)
    block_rows = N_COL * ROWS_DEV
    slots = jnp.arange(TILES_DEV, dtype=jnp.int32)

    def per_row(r):

        def per_col(total, c):
            cols = grid[:, c].reshape(N_ROW * ROWS_DEV // TILE, TILE, EMB)
            picked = cols[tile_col[r, c]].astype(jnp.float32)
            weights = tile_values[r, c].astype(jnp.float32)
            prod = jnp.einsum('tij,tjk->tik', weights, picked)
            live = slots < tile_count[r, c]
            prod = jnp.where(live[:, None, None], prod, jnp.float32(0.0))
            sums = jax.ops.segment_sum(prod, tile_row[r, c], num_segments=block_rows // TILE)
            return (total + sums.reshape(block_rows, EMB), None)
        total, _ = lax.scan(per_col, jnp.zeros((block_rows, EMB), jnp.float32), jnp.arange(N_COL, dtype=jnp.int32))
        return total
    return lax.map(per_row, jnp.arange(N_ROW, dtype=jnp.int32)).reshape(N_ROW * N_COL * ROWS_DEV, EMB)

def reference(embed, degree, tile_row, tile_col, tile_count, tile_values, new_rows, new_bucket, bucket_norm):
    scale = lax.rsqrt(degree.astype(jnp.float32))
    state = (scale[:, None] * embed.astype(jnp.float32)).astype(jnp.bfloat16)
    for hop in range(HOPS - 1):
        summed = one_hop(state, tile_row, tile_col, tile_count, tile_values)
        state = ((scale * scale)[:, None] * summed).astype(jnp.bfloat16)
    last = one_hop(state, tile_row, tile_col, tile_count, tile_values)
    picked = last[new_rows]
    target = bucket_norm[new_bucket]
    return target[:, None] * picked * lax.rsqrt(lax.optimization_barrier(jnp.sum(picked * picked, axis=1, keepdims=True)) + 1e-06)
```

```python
import functools

import jax
import jax.numpy as jnp
from jax import lax
from jax.experimental import pallas as pl
from jax.experimental.pallas import tpu as pltpu
from jax.sharding import PartitionSpec as P

HOPS = 3
TILE = 128
ROW_TILES = 64
PIECE = 4
SLOTS = 256
PAIRS = 160
NEW = 256
UNROLL = 4
MESH = pl.DeviceIdType.MESH


def kernel(
    slot_a, slot_b, col_a, col_b, keep, last, state_ref, scale2_ref, rows_ref, tiles_ref,
    out_ref,
    tiles, state0, state1, state2, sums, block, send1, recv1, send2, recv2, own, rows_all, rows_smem, rows_tmp,
    pick1, pickr1, pick2, pickr2,
    tiles_sem, rows_sem, ag_send, ag_recv, s1_send, s1_recv, s2_send, s2_recv, nr_send, nr_recv,
):
    gathered = (state0, state1, state2)
    row = lax.axis_index("row")
    col = lax.axis_index("col")
    z_lo = col // 8
    x = (col // 2) % 4
    core = col % 2

    load = pltpu.make_async_copy(tiles_ref, tiles.at[pl.ds(0, SLOTS)], tiles_sem)
    load.start()

    def row_peer(j):
        z_hi = (row // 4 + j // 4) % 2
        y = (row % 4 + j % 4) % 4
        return {"row": z_hi * 4 + y, "col": col}

    def col_at(j, k):
        return ((z_lo + j // 4) % 2) * 8 + ((x + j % 4) % 4) * 2 + k

    sibling = {"row": row, "col": col + 1 - 2 * core}

    barrier = pltpu.get_barrier_semaphore()
    for j in range(1, 8):
        pl.semaphore_signal(barrier, inc=1, device_id=row_peer(j), device_id_type=MESH)
    for j in range(1, 16):
        peer = {"row": row, "col": (col + j) % 16}
        pl.semaphore_signal(barrier, inc=1, device_id=peer, device_id_type=MESH)
    tiles[SLOTS] = jnp.zeros((TILE, TILE), jnp.bfloat16)
    sums[PAIRS] = jnp.zeros((TILE, TILE), jnp.float32)
    rows_all[col] = rows_ref[...]
    state0[pl.ds(row * PIECE, PIECE)] = state_ref[...]
    pl.semaphore_wait(barrier, 22)

    def remote(src, dst, send, recv, peer):
        copy = pltpu.make_async_remote_copy(
            src_ref=src, dst_ref=dst, send_sem=send, recv_sem=recv,
            device_id=peer, device_id_type=MESH,
        )
        copy.start()
        return copy

    ORDER = (6, 5, 7, 4, 2, 1, 3)

    def spread(hop):
        copies = []
        for j in ORDER:
            mine = gathered[hop].at[pl.ds(row * PIECE, PIECE)]
            copies.append(remote(mine, mine, ag_send.at[hop, j], ag_recv.at[hop, j], row_peer(j)))
        return copies

    def wait_all(copies):
        for copy in copies:
            copy.wait()

    pending = spread(0)
    row_copies = [
        remote(
            rows_all.at[col], rows_all.at[col], nr_send.at[j], nr_recv.at[j],
            {"row": row, "col": (col + j) % 16},
        )
        for j in range(1, 16)
    ]
    load.wait()
    wait_all(row_copies)
    to_smem = pltpu.make_async_copy(rows_all, rows_smem, rows_sem)
    to_smem.start()
    to_smem.wait()

    for hop in range(HOPS):
        wait_all(pending)

        def step(i, acc):
            for u in range(UNROLL):
                p = i * UNROLL + u
                lhs = jnp.concatenate([tiles[slot_a[p]], tiles[slot_b[p]]], axis=1)
                state = gathered[hop]
                rhs = jnp.concatenate([state[col_a[p]], state[col_b[p]]], axis=0)
                prod = jnp.dot(lhs, rhs, preferred_element_type=jnp.float32)
                acc = prod + jnp.where(keep[p] > 0, acc, jnp.float32(0.0))
                sums[p] = acc
            return acc

        lax.fori_loop(0, PAIRS // UNROLL, step, jnp.zeros((TILE, TILE), jnp.float32))

        if hop < HOPS - 1:
            first = []
            for j in ORDER + (0,):

                def fill(t, _, j=j):
                    r = col_at(j, 1 - core) * PIECE + t
                    send1[hop, j, t] = sums[last[r]].astype(jnp.bfloat16)
                    return 0

                lax.fori_loop(0, PIECE, fill, 0)
                first.append(
                    remote(send1.at[hop, j], recv1.at[hop, j], s1_send.at[hop, j],
                           s1_recv.at[hop, j], sibling)
                )
            second = []
            for copy, j in zip(first, ORDER + (0,)):
                copy.wait()

                def both(t, _, j=j):
                    r = col_at(j, core) * PIECE + t
                    value = sums[last[r]] + recv1[hop, j, t].astype(jnp.float32)
                    if j == 0:
                        own[t] = value
                    else:
                        send2[hop, j, t] = value.astype(jnp.bfloat16)
                    return 0

                lax.fori_loop(0, PIECE, both, 0)
                if j:
                    second.append(
                        remote(send2.at[hop, j], recv2.at[hop, j], s2_send.at[hop, j],
                               s2_recv.at[hop, j], {"row": row, "col": col_at(j, core)})
                    )
            wait_all(second)

            def reduce(t, _):
                total = own[t]
                for j in range(1, 8):
                    total = total + recv2[hop, j, t].astype(jnp.float32)
                gathered[hop + 1][row * PIECE + t] = (scale2_ref[t] * total).astype(jnp.bfloat16)
                return 0

            lax.fori_loop(0, PIECE, reduce, 0)
            pending = spread(hop + 1)

    def dense(r, _):
        block[pl.ds(pl.multiple_of(r * TILE, TILE), TILE), :] = sums[last[r]]
        return 0

    lax.fori_loop(0, ROW_TILES, dense, 0)

    def pick(c):
        def some(i, _):
            for u in range(16):
                n = i * 16 + u
                rows_tmp[pl.ds(n, 1), :] = block[pl.ds(rows_smem[c, 0, n], 1), :]
            return 0

        lax.fori_loop(0, NEW // 16, some, 0)
        return rows_tmp[...]

    first = []
    for j in ORDER + (0,):
        pick1[j] = pick(col_at(j, 1 - core)).astype(jnp.bfloat16)
        first.append(remote(pick1.at[j], pickr1.at[j], s1_send.at[2, j], s1_recv.at[2, j], sibling))
    second = []
    for copy, j in zip(first, ORDER + (0,)):
        mine = pick(col_at(j, core))
        copy.wait()
        value = mine + pickr1[j].astype(jnp.float32)
        if j == 0:
            out_ref[...] = value
        else:
            pick2[j] = value.astype(jnp.bfloat16)
            second.append(
                remote(pick2.at[j], pickr2.at[j], s2_send.at[2, j], s2_recv.at[2, j],
                       {"row": row, "col": col_at(j, core)})
            )
    wait_all(second)
    total = out_ref[...]
    for j in range(1, 8):
        total = total + pickr2[j].astype(jnp.float32)
    out_ref[...] = total


def tables(tile_row, tile_col, tile_count):
    slots = jnp.arange(SLOTS, dtype=jnp.int32)
    rows = jnp.arange(ROW_TILES, dtype=jnp.int32)
    pairs = jnp.arange(PAIRS, dtype=jnp.int32)
    live = slots < tile_count
    key = jnp.where(live, tile_row, ROW_TILES)
    before = jnp.sum((key[None, :] == key[:, None]) & (slots[None, :] < slots[:, None]), axis=1)
    count = jnp.sum(key[None, :] == rows[:, None], axis=1)
    halves = (count + 1) // 2
    start = jnp.sum(jnp.where(rows[None, :] < rows[:, None], halves[None, :], 0), axis=1)
    slot_start = jnp.sum(jnp.where(rows[None, :] < key[:, None], halves[None, :], 0), axis=1)
    place = jnp.where(live, 2 * (slot_start + before // 2) + before % 2, 2 * PAIRS)

    def at(half):
        hit = place[None, :] == (2 * pairs + half)[:, None]
        any_hit = jnp.any(hit, axis=1)
        slot = jnp.where(any_hit, jnp.sum(jnp.where(hit, slots[None, :], 0), axis=1), SLOTS)
        return slot, jnp.sum(jnp.where(hit, tile_col[None, :], 0), axis=1)

    slot_a, col_a = at(0)
    slot_b, col_b = at(1)
    starts_here = jnp.any((start[None, :] == pairs[:, None]) & (count > 0)[None, :], axis=1)
    keep = jnp.where(starts_here, 0, 1)
    last = jnp.where(count > 0, start + halves - 1, PAIRS)
    i32 = jnp.int32
    return tuple(v.astype(i32) for v in (slot_a, slot_b, col_a, col_b, keep, last))


def local(
    embed, degree, tile_row, tile_col, tile_count, tile_values, new_rows, new_bucket, bucket_norm
):
    scale = lax.rsqrt(degree.astype(jnp.float32))
    state = (scale[:, None] * embed.astype(jnp.float32)).astype(jnp.bfloat16)
    state = state.reshape(PIECE, TILE, TILE)
    scale2 = jnp.broadcast_to((scale * scale)[:, None], embed.shape).reshape(PIECE, TILE, TILE)
    ints = tables(tile_row[0, 0], tile_col[0, 0], tile_count[0, 0])
    local_ids = (new_rows - lax.axis_index("row") * (ROW_TILES * TILE)).reshape(1, NEW)

    smem = pl.BlockSpec(memory_space=pltpu.SMEM)
    vmem = pl.BlockSpec(memory_space=pltpu.VMEM)
    bf16, f32 = jnp.bfloat16, jnp.float32
    dma = pltpu.SemaphoreType.DMA
    picked = pl.pallas_call(
        kernel,
        name="propagate",
        out_shape=jax.ShapeDtypeStruct((NEW, TILE), f32),
        in_specs=[smem] * 6 + [vmem, vmem, vmem, pl.BlockSpec(memory_space=pl.ANY)],
        out_specs=vmem,
        scratch_shapes=[
            pltpu.VMEM((SLOTS + 1, TILE, TILE), bf16),
            pltpu.VMEM((32, TILE, TILE), bf16),
            pltpu.VMEM((32, TILE, TILE), bf16),
            pltpu.VMEM((32, TILE, TILE), bf16),
            pltpu.VMEM((PAIRS + 1, TILE, TILE), f32),
            pltpu.VMEM((ROW_TILES * TILE, TILE), f32),
            pltpu.VMEM((2, 8, PIECE, TILE, TILE), bf16),
            pltpu.VMEM((2, 8, PIECE, TILE, TILE), bf16),
            pltpu.VMEM((2, 8, PIECE, TILE, TILE), bf16),
            pltpu.VMEM((2, 8, PIECE, TILE, TILE), bf16),
            pltpu.VMEM((PIECE, TILE, TILE), f32),
            pltpu.VMEM((16, 1, NEW), jnp.int32),
            pltpu.SMEM((16, 1, NEW), jnp.int32),
            pltpu.VMEM((NEW, TILE), f32),
            pltpu.VMEM((8, NEW, TILE), bf16),
            pltpu.VMEM((8, NEW, TILE), bf16),
            pltpu.VMEM((8, NEW, TILE), bf16),
            pltpu.VMEM((8, NEW, TILE), bf16),
            dma, dma,
            dma((HOPS, 8)), dma((HOPS, 8)), dma((HOPS, 8)), dma((HOPS, 8)),
            dma((HOPS, 8)), dma((HOPS, 8)), dma((16,)), dma((16,)),
        ],
        compiler_params=pltpu.CompilerParams(
            collective_id=0, has_side_effects=True, vmem_limit_bytes=56 << 20
        ),
    )(*ints, state, scale2, local_ids, tile_values[0, 0])

    buckets = jnp.arange(bucket_norm.shape[0], dtype=jnp.int32)
    target = jnp.sum(
        jnp.where(new_bucket[:, None] == buckets[None, :], bucket_norm[None, :], jnp.float32(0.0)),
        axis=1,
    )
    return (
        target[:, None]
        * picked
        * lax.rsqrt(jnp.sum(picked * picked, axis=1, keepdims=True) + 1e-06)
    )


def solution(mesh):
    in_specs = (
        P(("row", "col"), None),
        P(("row", "col")),
        P("row", "col", None),
        P("row", "col", None),
        P("row", "col"),
        P("row", "col", None, None, None),
        P(("row", "col")),
        P(("row", "col")),
        P(),
    )
    out_specs = P(("row", "col"), None)
    return jax.shard_map(local, mesh=mesh, in_specs=in_specs, out_specs=out_specs, check_vma=False)
```

```python
import functools

import jax
import jax.numpy as jnp
from jax import lax
from jax.experimental import pallas as pl
from jax.experimental.pallas import tpu as pltpu
from jax.sharding import PartitionSpec as P

HOPS = 3
TILE = 128
ROW_TILES = 64
PIECE = 4
SLOTS = 256
PAIRS = 160
NEW = 256
UNROLL = 32
MESH = pl.DeviceIdType.MESH


def kernel(
    slot_a, slot_b, col_a, col_b, keep, last, state_ref, scale2_ref, rows_ref, tiles_ref,
    out_ref,
    tiles, state0, state1, state2, sums, block, send1, recv1, send2, recv2, own, rows_all, rows_smem, rows_tmp,
    pick1, pickr1, pick2, pickr2,
    tiles_sem, rows_sem, ag_send, ag_recv, s1_send, s1_recv, s2_send, s2_recv, nr_send, nr_recv,
    p1_send, p1_recv, p2_send, p2_recv,
):
    gathered = (state0, state1, state2)
    row = lax.axis_index("row")
    col = lax.axis_index("col")
    z_lo = col // 8
    x = (col // 2) % 4
    core = col % 2

    load = pltpu.make_async_copy(tiles_ref, tiles.at[pl.ds(0, SLOTS)], tiles_sem)
    load.start()

    def row_peer(j):
        z_hi = (row // 4 + j // 4) % 2
        y = (row % 4 + j % 4) % 4
        return {"row": z_hi * 4 + y, "col": col}

    def col_at(j, k):
        return ((z_lo + j // 4) % 2) * 8 + ((x + j % 4) % 4) * 2 + k

    sibling = {"row": row, "col": col + 1 - 2 * core}

    barrier = pltpu.get_barrier_semaphore()
    for j in range(1, 8):
        pl.semaphore_signal(barrier, inc=1, device_id=row_peer(j), device_id_type=MESH)
    for j in range(1, 16):
        peer = {"row": row, "col": (col + j) % 16}
        pl.semaphore_signal(barrier, inc=1, device_id=peer, device_id_type=MESH)
    tiles[SLOTS] = jnp.zeros((TILE, TILE), jnp.bfloat16)
    sums[PAIRS] = jnp.zeros((TILE, TILE), jnp.float32)
    rows_all[col] = rows_ref[...]
    state0[pl.ds(row * PIECE, PIECE)] = state_ref[...]
    pl.semaphore_wait(barrier, 22)

    def remote(src, dst, send, recv, peer):
        copy = pltpu.make_async_remote_copy(
            src_ref=src, dst_ref=dst, send_sem=send, recv_sem=recv,
            device_id=peer, device_id_type=MESH,
        )
        copy.start()
        return copy

    def gather_start(hop, q):
        mine = gathered[hop].at[row * PIECE + q]
        return [
            remote(mine, mine, ag_send.at[hop, q, j], ag_recv.at[hop, q, j], row_peer(peer))
            for j, peer in enumerate((4, 2, 1, 3))
        ]

    def gather_forward(hop, q, copies):
        copies[0].wait_recv()
        theirs = gathered[hop].at[((row + 4) % 8) * PIECE + q]
        return [
            remote(theirs, theirs, ag_send.at[hop, q, j], ag_recv.at[hop, q, j], row_peer(peer))
            for j, peer in enumerate((2, 1, 3), 4)
        ]

    def gather_end(copies, forwards):
        for some in copies:
            some[0].wait_send()
            for copy in some[1:]:
                copy.wait()
        for some in forwards:
            for copy in some:
                copy.wait()

    row_copies = [
        remote(
            rows_all.at[col], rows_all.at[col], nr_send.at[j], nr_recv.at[j],
            {"row": row, "col": (col + j) % 16},
        )
        for j in range(1, 16)
    ]
    copies = [gather_start(0, q) for q in range(PIECE)]
    forwards = [gather_forward(0, q, copies[q]) for q in range(PIECE)]
    load.wait()
    for copy in row_copies:
        copy.wait()
    to_smem = pltpu.make_async_copy(rows_all, rows_smem, rows_sem)
    to_smem.start()
    to_smem.wait()

    ORDER = (6, 5, 7, 4, 2, 1, 3)
    for hop in range(HOPS):
        gather_end(copies, forwards)
        state = gathered[hop]

        def step(i, acc):
            for u in range(UNROLL):
                p = i * UNROLL + u
                lhs = jnp.concatenate([tiles[slot_a[p]], tiles[slot_b[p]]], axis=1)
                rhs = jnp.concatenate([state[col_a[p]], state[col_b[p]]], axis=0)
                prod = jnp.dot(lhs, rhs, preferred_element_type=jnp.float32)
                acc = prod + jnp.where(keep[p] > 0, acc, jnp.float32(0.0))
                sums[p] = acc
            return acc

        lax.fori_loop(0, PAIRS // UNROLL, step, jnp.zeros((TILE, TILE), jnp.float32))
        if hop == HOPS - 1:
            break

        def fill(q):
            for j in range(8):
                r = col_at(j, 1 - core) * PIECE + q
                send1[hop, q, j] = sums[last[r]].astype(jnp.bfloat16)
            return remote(send1.at[hop, q], recv1.at[hop, q], s1_send.at[hop, q],
                          s1_recv.at[hop, q], sibling)

        def both(q, copy):
            copy.wait()
            sent = []
            for j in ORDER + (0,):
                r = col_at(j, core) * PIECE + q
                value = sums[last[r]] + recv1[hop, q, j].astype(jnp.float32)
                if j == 0:
                    own[q] = value
                else:
                    send2[hop, q, j] = value.astype(jnp.bfloat16)
                    sent.append(
                        remote(send2.at[hop, q, j], recv2.at[hop, q, j], s2_send.at[hop, q, j],
                               s2_recv.at[hop, q, j], {"row": row, "col": col_at(j, core)})
                    )
            return sent

        def reduce(q, sent):
            total = own[q]
            for copy in sent:
                copy.wait()
            for j in range(1, 8):
                total = total + recv2[hop, q, j].astype(jnp.float32)
            gathered[hop + 1][row * PIECE + q] = (scale2_ref[q] * total).astype(jnp.bfloat16)
            return gather_start(hop + 1, q)

        first = [fill(0), fill(1)]
        second = [both(0, first[0])]
        for q in range(2, PIECE):
            first.append(fill(q))
            second.append(both(q - 1, first[q - 1]))
        second.append(both(PIECE - 1, first[PIECE - 1]))
        copies = [reduce(0, second[0])]
        forwards = []
        for q in range(1, PIECE):
            copies.append(reduce(q, second[q]))
            forwards.append(gather_forward(hop + 1, q - 1, copies[q - 1]))
        forwards.append(gather_forward(hop + 1, PIECE - 1, copies[PIECE - 1]))

    def dense(r, _):
        block[pl.ds(pl.multiple_of(r * TILE, TILE), TILE), :] = sums[last[r]]
        return 0

    lax.fori_loop(0, ROW_TILES, dense, 0)

    def pick(c):
        def some(i, _):
            for u in range(16):
                n = i * 16 + u
                rows_tmp[pl.ds(n, 1), :] = block[pl.ds(rows_smem[c, 0, n], 1), :]
            return 0

        lax.fori_loop(0, NEW // 16, some, 0)
        return rows_tmp[...]

    first = []
    for j in ORDER + (0,):
        pick1[j] = pick(col_at(j, 1 - core)).astype(jnp.bfloat16)
        first.append(remote(pick1.at[j], pickr1.at[j], p1_send.at[j], p1_recv.at[j], sibling))
    second = []
    for copy, j in zip(first, ORDER + (0,)):
        mine = pick(col_at(j, core))
        copy.wait()
        value = mine + pickr1[j].astype(jnp.float32)
        if j == 0:
            out_ref[...] = value
        else:
            pick2[j] = value.astype(jnp.bfloat16)
            second.append(
                remote(pick2.at[j], pickr2.at[j], p2_send.at[j], p2_recv.at[j],
                       {"row": row, "col": col_at(j, core)})
            )
    for copy in second:
        copy.wait()
    total = out_ref[...]
    for j in range(1, 8):
        total = total + pickr2[j].astype(jnp.float32)
    out_ref[...] = total


def tables(tile_row, tile_col, tile_count):
    slots = jnp.arange(SLOTS, dtype=jnp.int32)
    rows = jnp.arange(ROW_TILES, dtype=jnp.int32)
    pairs = jnp.arange(PAIRS, dtype=jnp.int32)
    live = slots < tile_count
    key = jnp.where(live, tile_row, ROW_TILES)
    before = jnp.sum((key[None, :] == key[:, None]) & (slots[None, :] < slots[:, None]), axis=1)
    count = jnp.sum(key[None, :] == rows[:, None], axis=1)
    halves = (count + 1) // 2
    start = jnp.sum(jnp.where(rows[None, :] < rows[:, None], halves[None, :], 0), axis=1)
    slot_start = jnp.sum(jnp.where(rows[None, :] < key[:, None], halves[None, :], 0), axis=1)
    place = jnp.where(live, 2 * (slot_start + before // 2) + before % 2, 2 * PAIRS)

    def at(half):
        hit = place[None, :] == (2 * pairs + half)[:, None]
        any_hit = jnp.any(hit, axis=1)
        slot = jnp.where(any_hit, jnp.sum(jnp.where(hit, slots[None, :], 0), axis=1), SLOTS)
        return slot, jnp.sum(jnp.where(hit, tile_col[None, :], 0), axis=1)

    slot_a, col_a = at(0)
    slot_b, col_b = at(1)
    starts_here = jnp.any((start[None, :] == pairs[:, None]) & (count > 0)[None, :], axis=1)
    keep = jnp.where(starts_here, 0, 1)
    last = jnp.where(count > 0, start + halves - 1, PAIRS)
    i32 = jnp.int32
    return tuple(v.astype(i32) for v in (slot_a, slot_b, col_a, col_b, keep, last))


def local(
    embed, degree, tile_row, tile_col, tile_count, tile_values, new_rows, new_bucket, bucket_norm
):
    scale = lax.rsqrt(degree.astype(jnp.float32))
    state = (scale[:, None] * embed.astype(jnp.float32)).astype(jnp.bfloat16)
    state = state.reshape(PIECE, TILE, TILE)
    scale2 = jnp.broadcast_to((scale * scale)[:, None], embed.shape).reshape(PIECE, TILE, TILE)
    ints = tables(tile_row[0, 0], tile_col[0, 0], tile_count[0, 0])
    local_ids = (new_rows - lax.axis_index("row") * (ROW_TILES * TILE)).reshape(1, NEW)

    smem = pl.BlockSpec(memory_space=pltpu.SMEM)
    vmem = pl.BlockSpec(memory_space=pltpu.VMEM)
    bf16, f32 = jnp.bfloat16, jnp.float32
    dma = pltpu.SemaphoreType.DMA
    picked = pl.pallas_call(
        kernel,
        name="propagate",
        out_shape=jax.ShapeDtypeStruct((NEW, TILE), f32),
        in_specs=[smem] * 6 + [vmem, vmem, vmem, pl.BlockSpec(memory_space=pl.ANY)],
        out_specs=vmem,
        scratch_shapes=[
            pltpu.VMEM((SLOTS + 1, TILE, TILE), bf16),
            pltpu.VMEM((32, TILE, TILE), bf16),
            pltpu.VMEM((32, TILE, TILE), bf16),
            pltpu.VMEM((32, TILE, TILE), bf16),
            pltpu.VMEM((PAIRS + 1, TILE, TILE), f32),
            pltpu.VMEM((ROW_TILES * TILE, TILE), f32),
            pltpu.VMEM((2, PIECE, 8, TILE, TILE), bf16),
            pltpu.VMEM((2, PIECE, 8, TILE, TILE), bf16),
            pltpu.VMEM((2, PIECE, 8, TILE, TILE), bf16),
            pltpu.VMEM((2, PIECE, 8, TILE, TILE), bf16),
            pltpu.VMEM((PIECE, TILE, TILE), f32),
            pltpu.VMEM((16, 1, NEW), jnp.int32),
            pltpu.SMEM((16, 1, NEW), jnp.int32),
            pltpu.VMEM((NEW, TILE), f32),
            pltpu.VMEM((8, NEW, TILE), bf16),
            pltpu.VMEM((8, NEW, TILE), bf16),
            pltpu.VMEM((8, NEW, TILE), bf16),
            pltpu.VMEM((8, NEW, TILE), bf16),
            dma, dma,
            dma((HOPS, PIECE, 7)), dma((HOPS, PIECE, 7)), dma((2, PIECE)), dma((2, PIECE)),
            dma((2, PIECE, 8)), dma((2, PIECE, 8)), dma((16,)), dma((16,)),
            dma((8,)), dma((8,)), dma((8,)), dma((8,)),
        ],
        compiler_params=pltpu.CompilerParams(
            collective_id=0, has_side_effects=True, vmem_limit_bytes=56 << 20
        ),
    )(*ints, state, scale2, local_ids, tile_values[0, 0])

    buckets = jnp.arange(bucket_norm.shape[0], dtype=jnp.int32)
    target = jnp.sum(
        jnp.where(new_bucket[:, None] == buckets[None, :], bucket_norm[None, :], jnp.float32(0.0)),
        axis=1,
    )
    return (
        target[:, None]
        * picked
        * lax.rsqrt(jnp.sum(picked * picked, axis=1, keepdims=True) + 1e-06)
    )


def solution(mesh):
    in_specs = (
        P(("row", "col"), None),
        P(("row", "col")),
        P("row", "col", None),
        P("row", "col", None),
        P("row", "col"),
        P("row", "col", None, None, None),
        P(("row", "col")),
        P(("row", "col")),
        P(),
    )
    out_specs = P(("row", "col"), None)
    return jax.shard_map(local, mesh=mesh, in_specs=in_specs, out_specs=out_specs, check_vma=False)
```

```python
import functools

import jax
import jax.numpy as jnp
from jax import lax
from jax.experimental import pallas as pl
from jax.experimental.pallas import tpu as pltpu
from jax.sharding import PartitionSpec as P

HOPS = 3
TILE = 128
ROW_TILES = 64
PIECE = 4
SLOTS = 256
PAIRS = 160
NEW = 256
UNROLL = 32
MESH = pl.DeviceIdType.MESH


def kernel(
    count_ref, norm_ref, embed_ref, degree_ref, trow_ref, tcol_ref, rows_ref, bucket_ref, tiles_ref,
    out_ref,
    table, table_smem, scale2_ref, target,
    tiles, state0, state1, state2, sums, block, send1, recv1, send2, recv2, own, rows_all, rows_smem, rows_tmp,
    pick1, pickr1, pick2, pickr2,
    tiles_sem, rows_sem, table_sem, ag_send, ag_recv, s1_send, s1_recv, s2_send, s2_recv, nr_send, nr_recv,
    p1_send, p1_recv, p2_send, p2_recv,
):
    gathered = (state0, state1, state2)
    row = lax.axis_index("row")
    col = lax.axis_index("col")
    z_lo = col // 8
    x = (col // 2) % 4
    core = col % 2

    load = pltpu.make_async_copy(tiles_ref, tiles.at[pl.ds(0, SLOTS)], tiles_sem)
    load.start()

    def row_peer(j):
        z_hi = (row // 4 + j // 4) % 2
        y = (row % 4 + j % 4) % 4
        return {"row": z_hi * 4 + y, "col": col}

    def col_at(j, k):
        return ((z_lo + j // 4) % 2) * 8 + ((x + j % 4) % 4) * 2 + k

    sibling = {"row": row, "col": col + 1 - 2 * core}

    barrier = pltpu.get_barrier_semaphore()
    for j in range(1, 8):
        pl.semaphore_signal(barrier, inc=1, device_id=row_peer(j), device_id_type=MESH)
    for j in range(1, 16):
        peer = {"row": row, "col": (col + j) % 16}
        pl.semaphore_signal(barrier, inc=1, device_id=peer, device_id_type=MESH)

    def column(values, width=None):
        n = values.shape[1]
        return jnp.transpose(jnp.broadcast_to(values, (width or n, n)))

    scale = lax.rsqrt(degree_ref[...].astype(jnp.float32))
    for t in range(PIECE):
        wide = column(scale[t : t + 1], TILE)
        state0[row * PIECE + t] = (wide * embed_ref[t].astype(jnp.float32)).astype(jnp.bfloat16)
        scale2_ref[t] = wide * wide
    tiles[SLOTS] = jnp.zeros((TILE, TILE), jnp.bfloat16)
    sums[PAIRS] = jnp.zeros((TILE, TILE), jnp.float32)
    rows_all[col] = jnp.clip(
        rows_ref[...] - row * (ROW_TILES * TILE), 0, ROW_TILES * TILE - 1
    )
    pl.semaphore_wait(barrier, 22)

    def remote(src, dst, send, recv, peer):
        copy = pltpu.make_async_remote_copy(
            src_ref=src, dst_ref=dst, send_sem=send, recv_sem=recv,
            device_id=peer, device_id_type=MESH,
        )
        copy.start()
        return copy

    def gather_start(hop, q):
        mine = gathered[hop].at[row * PIECE + q]
        return [
            remote(mine, mine, ag_send.at[hop, q, j], ag_recv.at[hop, q, j], row_peer(peer))
            for j, peer in enumerate((4, 2, 1, 3))
        ]

    def gather_forward(hop, q, copies):
        copies[0].wait_recv()
        theirs = gathered[hop].at[((row + 4) % 8) * PIECE + q]
        return [
            remote(theirs, theirs, ag_send.at[hop, q, j], ag_recv.at[hop, q, j], row_peer(peer))
            for j, peer in enumerate((2, 1, 3), 4)
        ]

    def gather_end(copies, forwards):
        for some in copies:
            some[0].wait_send()
            for copy in some[1:]:
                copy.wait()
        for some in forwards:
            for copy in some:
                copy.wait()

    row_copies = [
        remote(
            rows_all.at[col], rows_all.at[col], nr_send.at[j], nr_recv.at[j],
            {"row": row, "col": (col + j) % 16},
        )
        for j in range(1, 16)
    ]
    copies = [gather_start(0, q) for q in range(PIECE)]

    ids = lax.broadcasted_iota(jnp.int32, (1, SLOTS), 1)
    live = ids < count_ref[0, 0]
    key = jnp.where(live, trow_ref[...], ROW_TILES)
    sub = lax.broadcasted_iota(jnp.int32, (SLOTS, SLOTS), 0)
    lane = lax.broadcasted_iota(jnp.int32, (SLOTS, SLOTS), 1)

    def count(mask):
        return jnp.sum(jnp.where(mask, 1, 0), axis=0, keepdims=True)

    before = count((column(key) == key) & (sub < lane))
    opener = column(jnp.where(before % 2 == 0, key, ROW_TILES))
    place_row = jnp.where(live, 2 * count(opener < key) + before, 4 * SLOTS)
    place = column(place_row)
    source = column(tcol_ref[...])

    def total_of(mask, values):
        return jnp.sum(jnp.where(mask, values, 0), axis=0, keepdims=True)

    for half in range(2):
        hit = place == 2 * lane + half
        table[half : half + 1, :] = jnp.clip(total_of(hit, sub - SLOTS) + SLOTS, 0, SLOTS)
        table[half + 2 : half + 3, :] = jnp.clip(total_of(hit, source), 0, 31)
    starts = column(jnp.where(before == 0, place_row, 4 * SLOTS))
    table[4:5, :] = 1 - count(starts == 2 * lane)
    upto = count(opener <= lane)
    table[5:6, :] = jnp.clip(
        jnp.where(count(opener == lane) > 0, upto - 1, PAIRS), 0, PAIRS
    )
    to_table = pltpu.make_async_copy(table, table_smem, table_sem)
    to_table.start()

    forwards = [gather_forward(0, q, copies[q]) for q in range(PIECE)]
    for t in range(NEW // TILE):
        chosen = jnp.zeros((1, TILE), jnp.float32)
        for b in range(16):
            chosen = jnp.where(bucket_ref[t : t + 1] == b, norm_ref[b], chosen)
        target[t * TILE : (t + 1) * TILE] = column(chosen, TILE)
    load.wait()
    to_table.wait()
    for copy in row_copies:
        copy.wait()
    to_smem = pltpu.make_async_copy(rows_all, rows_smem, rows_sem)
    to_smem.start()
    to_smem.wait()

    ORDER = (6, 5, 7, 4, 2, 1, 3)
    for hop in range(HOPS):
        gather_end(copies, forwards)
        state = gathered[hop]

        def step(i, acc):
            for u in range(UNROLL):
                p = i * UNROLL + u
                lhs = jnp.concatenate([tiles[table_smem[0, p]], tiles[table_smem[1, p]]], axis=1)
                rhs = jnp.concatenate([state[table_smem[2, p]], state[table_smem[3, p]]], axis=0)
                prod = jnp.dot(lhs, rhs, preferred_element_type=jnp.float32)
                acc = prod + jnp.where(table_smem[4, p] > 0, acc, jnp.float32(0.0))
                sums[p] = acc
            return acc

        lax.fori_loop(0, PAIRS // UNROLL, step, jnp.zeros((TILE, TILE), jnp.float32))
        if hop == HOPS - 1:
            break

        def fill(q):
            for j in range(8):
                r = col_at(j, 1 - core) * PIECE + q
                send1[hop, q, j] = sums[table_smem[5, r]].astype(jnp.bfloat16)
            return remote(send1.at[hop, q], recv1.at[hop, q], s1_send.at[hop, q],
                          s1_recv.at[hop, q], sibling)

        def both(q, copy):
            copy.wait()
            sent = []
            for j in ORDER + (0,):
                r = col_at(j, core) * PIECE + q
                value = sums[table_smem[5, r]] + recv1[hop, q, j].astype(jnp.float32)
                if j == 0:
                    own[q] = value
                else:
                    send2[hop, q, j] = value.astype(jnp.bfloat16)
                    sent.append(
                        remote(send2.at[hop, q, j], recv2.at[hop, q, j], s2_send.at[hop, q, j],
                               s2_recv.at[hop, q, j], {"row": row, "col": col_at(j, core)})
                    )
            return sent

        def reduce(q, sent):
            total = own[q]
            for copy in sent:
                copy.wait()
            for j in range(1, 8):
                total = total + recv2[hop, q, j].astype(jnp.float32)
            gathered[hop + 1][row * PIECE + q] = (scale2_ref[q] * total).astype(jnp.bfloat16)
            return gather_start(hop + 1, q)

        first = [fill(0), fill(1)]
        second = [both(0, first[0])]
        for q in range(2, PIECE):
            first.append(fill(q))
            second.append(both(q - 1, first[q - 1]))
        second.append(both(PIECE - 1, first[PIECE - 1]))
        copies = [reduce(0, second[0])]
        forwards = []
        for q in range(1, PIECE):
            copies.append(reduce(q, second[q]))
            forwards.append(gather_forward(hop + 1, q - 1, copies[q - 1]))
        forwards.append(gather_forward(hop + 1, PIECE - 1, copies[PIECE - 1]))

    def dense(r, _):
        block[pl.ds(pl.multiple_of(r * TILE, TILE), TILE), :] = sums[table_smem[5, r]]
        return 0

    lax.fori_loop(0, ROW_TILES, dense, 0)

    def pick(c):
        def some(i, _):
            for u in range(16):
                n = i * 16 + u
                rows_tmp[pl.ds(n, 1), :] = block[pl.ds(rows_smem[c, 0, n], 1), :]
            return 0

        lax.fori_loop(0, NEW // 16, some, 0)
        return rows_tmp[...]

    first = []
    for j in ORDER + (0,):
        pick1[j] = pick(col_at(j, 1 - core)).astype(jnp.bfloat16)
        first.append(remote(pick1.at[j], pickr1.at[j], p1_send.at[j], p1_recv.at[j], sibling))
    second = []
    for copy, j in zip(first, ORDER + (0,)):
        mine = pick(col_at(j, core))
        copy.wait()
        value = mine + pickr1[j].astype(jnp.float32)
        if j == 0:
            out_ref[...] = value
        else:
            pick2[j] = value.astype(jnp.bfloat16)
            second.append(
                remote(pick2.at[j], pickr2.at[j], p2_send.at[j], p2_recv.at[j],
                       {"row": row, "col": col_at(j, core)})
            )
    for copy in second:
        copy.wait()
    total = out_ref[...]
    for j in range(1, 8):
        total = total + pickr2[j].astype(jnp.float32)
    square = jnp.sum(total * total, axis=1, keepdims=True)
    out_ref[...] = target[...] * total * lax.rsqrt(square + 1e-06)


def local(
    embed, degree, tile_row, tile_col, tile_count, tile_values, new_rows, new_bucket, bucket_norm
):
    smem = pl.BlockSpec(memory_space=pltpu.SMEM)
    vmem = pl.BlockSpec(memory_space=pltpu.VMEM)
    bf16, f32 = jnp.bfloat16, jnp.float32
    dma = pltpu.SemaphoreType.DMA
    return pl.pallas_call(
        kernel,
        name="propagate",
        out_shape=jax.ShapeDtypeStruct((NEW, TILE), f32),
        in_specs=[smem] * 2 + [vmem] * 6 + [pl.BlockSpec(memory_space=pl.ANY)],
        out_specs=vmem,
        scratch_shapes=[
            pltpu.VMEM((8, SLOTS), jnp.int32),
            pltpu.SMEM((8, SLOTS), jnp.int32),
            pltpu.VMEM((PIECE, TILE, TILE), f32),
            pltpu.VMEM((NEW, TILE), f32),
            pltpu.VMEM((SLOTS + 1, TILE, TILE), bf16),
            pltpu.VMEM((32, TILE, TILE), bf16),
            pltpu.VMEM((32, TILE, TILE), bf16),
            pltpu.VMEM((32, TILE, TILE), bf16),
            pltpu.VMEM((PAIRS + 1, TILE, TILE), f32),
            pltpu.VMEM((ROW_TILES * TILE, TILE), f32),
            pltpu.VMEM((2, PIECE, 8, TILE, TILE), bf16),
            pltpu.VMEM((2, PIECE, 8, TILE, TILE), bf16),
            pltpu.VMEM((2, PIECE, 8, TILE, TILE), bf16),
            pltpu.VMEM((2, PIECE, 8, TILE, TILE), bf16),
            pltpu.VMEM((PIECE, TILE, TILE), f32),
            pltpu.VMEM((16, 1, NEW), jnp.int32),
            pltpu.SMEM((16, 1, NEW), jnp.int32),
            pltpu.VMEM((NEW, TILE), f32),
            pltpu.VMEM((8, NEW, TILE), bf16),
            pltpu.VMEM((8, NEW, TILE), bf16),
            pltpu.VMEM((8, NEW, TILE), bf16),
            pltpu.VMEM((8, NEW, TILE), bf16),
            dma, dma, dma,
            dma((HOPS, PIECE, 7)), dma((HOPS, PIECE, 7)), dma((2, PIECE)), dma((2, PIECE)),
            dma((2, PIECE, 8)), dma((2, PIECE, 8)), dma((16,)), dma((16,)),
            dma((8,)), dma((8,)), dma((8,)), dma((8,)),
        ],
        compiler_params=pltpu.CompilerParams(
            collective_id=0, has_side_effects=True, vmem_limit_bytes=56 << 20
        ),
    )(
        tile_count, bucket_norm, embed.reshape(PIECE, TILE, TILE), degree.reshape(PIECE, TILE),
        tile_row[0], tile_col[0], new_rows.reshape(1, NEW), new_bucket.reshape(NEW // TILE, TILE),
        tile_values[0, 0],
    )


def solution(mesh):
    in_specs = (
        P(("row", "col"), None),
        P(("row", "col")),
        P("row", "col", None),
        P("row", "col", None),
        P("row", "col"),
        P("row", "col", None, None, None),
        P(("row", "col")),
        P(("row", "col")),
        P(),
    )
    out_specs = P(("row", "col"), None)
    return jax.shard_map(local, mesh=mesh, in_specs=in_specs, out_specs=out_specs, check_vma=False)
```

```python
import functools

import jax
import jax.numpy as jnp
from jax import lax
from jax.experimental import pallas as pl
from jax.experimental.pallas import tpu as pltpu
from jax.sharding import PartitionSpec as P

HOPS = 3
TILE = 128
ROW_TILES = 64
PIECE = 4
SLOTS = 256
PAIRS = 160
NEW = 256
UNROLL = 32
CHUNKS = 2
CHUNK = PIECE // CHUNKS
Z_FIRST = (0,)
Y_FIRST = (0,)
DIRECT = ()
ORDER = (6, 5, 7, 4, 2, 1, 3)
SCHEDULE = tuple(
    (step[0], int(step[1])) for step in "f0 f1 a0 a1 b0 b1 r0 r1 g0 g1".split()
)
MESH = pl.DeviceIdType.MESH


def kernel(
    count_ref, norm_ref, embed_ref, degree_ref, trow_ref, tcol_ref, rows_ref, bucket_ref, tiles_ref,
    out_ref,
    table, table_smem, scale2_ref, target,
    tiles, state0, state1, state2, sums, block, send1, recv1, send2, recv2, send3, recv3, own, rows_all, rows_smem, rows_tmp,
    pick1, pickr1, pick2, pickr2,
    tiles_sem, rows_sem, table_sem, ag_send, ag_recv, s1_send, s1_recv, s2_send, s2_recv, s3_send, s3_recv, nr_send, nr_recv,
    p1_send, p1_recv, p2_send, p2_recv,
):
    gathered = (state0, state1, state2)
    row = lax.axis_index("row")
    col = lax.axis_index("col")
    z_lo = col // 8
    x = (col // 2) % 4
    core = col % 2

    load = pltpu.make_async_copy(tiles_ref, tiles.at[pl.ds(0, SLOTS)], tiles_sem)
    load.start()

    def row_peer(j):
        z_hi = (row // 4 + j // 4) % 2
        y = (row % 4 + j % 4) % 4
        return {"row": z_hi * 4 + y, "col": col}

    def col_at(j, k):
        return ((z_lo + j // 4) % 2) * 8 + ((x + j % 4) % 4) * 2 + k

    sibling = {"row": row, "col": col + 1 - 2 * core}

    barrier = pltpu.get_barrier_semaphore()
    for j in range(1, 8):
        pl.semaphore_signal(barrier, inc=1, device_id=row_peer(j), device_id_type=MESH)
    for j in range(1, 16):
        peer = {"row": row, "col": (col + j) % 16}
        pl.semaphore_signal(barrier, inc=1, device_id=peer, device_id_type=MESH)

    def column(values, width=None):
        n = values.shape[1]
        return jnp.transpose(jnp.broadcast_to(values, (width or n, n)))

    scale = lax.rsqrt(degree_ref[...].astype(jnp.float32))
    for t in range(PIECE):
        wide = column(scale[t : t + 1], TILE)
        state0[row * PIECE + t] = (wide * embed_ref[t].astype(jnp.float32)).astype(jnp.bfloat16)
        scale2_ref[t] = wide * wide
    tiles[SLOTS] = jnp.zeros((TILE, TILE), jnp.bfloat16)
    sums[PAIRS] = jnp.zeros((TILE, TILE), jnp.float32)
    rows_all[col] = jnp.clip(
        rows_ref[...] - row * (ROW_TILES * TILE), 0, ROW_TILES * TILE - 1
    )
    pl.semaphore_wait(barrier, 22)

    def remote(src, dst, send, recv, peer):
        copy = pltpu.make_async_remote_copy(
            src_ref=src, dst_ref=dst, send_sem=send, recv_sem=recv,
            device_id=peer, device_id_type=MESH,
        )
        copy.start()
        return copy

    def chunk(hop, who, q):
        return gathered[hop].at[pl.ds(who * PIECE + q * CHUNK, CHUNK)]

    def gather_start(hop, q):
        mine = chunk(hop, row, q)
        return [
            remote(mine, mine, ag_send.at[hop, q, j], ag_recv.at[hop, q, j], row_peer(peer))
            for j, peer in enumerate((4, 2, 1, 3) + ((6, 5, 7) if hop in DIRECT else ()))
        ]

    def gather_forward(hop, q, copies):
        sent = []
        if hop in DIRECT:
            return sent
        if q not in Y_FIRST:
            copies[0].wait_recv()
        for j, dy in ((1, 2), (2, 1), (3, 3)):
            if q in Y_FIRST:
                copies[j].wait_recv()
                theirs = chunk(hop, (row // 4) * 4 + (row + 4 - dy) % 4, q)
            else:
                theirs = chunk(hop, (row + 4) % 8, q)
            peer = row_peer(4 if q in Y_FIRST else dy)
            sent.append(remote(theirs, theirs, ag_send.at[hop, q, 3 + j],
                               ag_recv.at[hop, q, 3 + j], peer))
        return sent

    def gather_end(hop, copies, forwards):
        for q in range(CHUNKS):
            for j, copy in enumerate(copies[q]):
                copy.wait_send()
                if hop in DIRECT or (j == 0) == (q in Y_FIRST):
                    copy.wait_recv()
            for copy in forwards[q]:
                copy.wait()

    row_copies = [
        remote(
            rows_all.at[col], rows_all.at[col], nr_send.at[j], nr_recv.at[j],
            {"row": row, "col": (col + j) % 16},
        )
        for j in range(1, 16)
    ]
    copies = [gather_start(0, q) for q in range(CHUNKS)]

    ids = lax.broadcasted_iota(jnp.int32, (1, SLOTS), 1)
    live = ids < count_ref[0, 0]
    key = jnp.where(live, trow_ref[...], ROW_TILES)
    sub = lax.broadcasted_iota(jnp.int32, (SLOTS, SLOTS), 0)
    lane = lax.broadcasted_iota(jnp.int32, (SLOTS, SLOTS), 1)

    def count(mask):
        return jnp.sum(jnp.where(mask, 1, 0), axis=0, keepdims=True)

    before = count((column(key) == key) & (sub < lane))
    opener = column(jnp.where(before % 2 == 0, key, ROW_TILES))
    place_row = jnp.where(live, 2 * count(opener < key) + before, 4 * SLOTS)
    place = column(place_row)
    source = column(tcol_ref[...])

    def total_of(mask, values):
        return jnp.sum(jnp.where(mask, values, 0), axis=0, keepdims=True)

    for half in range(2):
        hit = place == 2 * lane + half
        table[half : half + 1, :] = jnp.clip(total_of(hit, sub - SLOTS) + SLOTS, 0, SLOTS)
        table[half + 2 : half + 3, :] = jnp.clip(total_of(hit, source), 0, 31)
    starts = column(jnp.where(before == 0, place_row, 4 * SLOTS))
    table[4:5, :] = 1 - count(starts == 2 * lane)
    upto = count(opener <= lane)
    table[5:6, :] = jnp.clip(
        jnp.where(count(opener == lane) > 0, upto - 1, PAIRS), 0, PAIRS
    )
    to_table = pltpu.make_async_copy(table, table_smem, table_sem)
    to_table.start()

    forwards = [gather_forward(0, q, copies[q]) for q in range(CHUNKS)]
    for t in range(NEW // TILE):
        chosen = jnp.zeros((1, TILE), jnp.float32)
        for b in range(16):
            chosen = jnp.where(bucket_ref[t : t + 1] == b, norm_ref[b], chosen)
        target[t * TILE : (t + 1) * TILE] = column(chosen, TILE)
    load.wait()
    to_table.wait()
    for copy in row_copies:
        copy.wait()
    to_smem = pltpu.make_async_copy(rows_all, rows_smem, rows_sem)
    to_smem.start()
    to_smem.wait()

    for hop in range(HOPS):
        gather_end(hop, copies, forwards)
        state = gathered[hop]

        def step(i, acc):
            for u in range(UNROLL):
                p = i * UNROLL + u
                lhs = jnp.concatenate([tiles[table_smem[0, p]], tiles[table_smem[1, p]]], axis=1)
                rhs = jnp.concatenate([state[table_smem[2, p]], state[table_smem[3, p]]], axis=0)
                prod = jnp.dot(lhs, rhs, preferred_element_type=jnp.float32)
                acc = prod + jnp.where(table_smem[4, p] > 0, acc, jnp.float32(0.0))
                sums[p] = acc
            return acc

        lax.fori_loop(0, PAIRS // UNROLL, step, jnp.zeros((TILE, TILE), jnp.float32))
        if hop == HOPS - 1:
            break

        def mine(j, k, q, t):
            return sums[table_smem[5, col_at(j, k) * PIECE + q * CHUNK + t]]

        def fill(q):
            for j in range(8):
                for t in range(CHUNK):
                    send1[hop, q, j, t] = mine(j, 1 - core, q, t).astype(jnp.bfloat16)
            return remote(send1.at[hop, q], recv1.at[hop, q], s1_send.at[hop, q],
                          s1_recv.at[hop, q], sibling)

        def value(q, j, t):
            return mine(j, core, q, t) + recv1[hop, q, j, t].astype(jnp.float32)

        def along(kind, q, part, slot, peer):
            src, dst, send, recv = kind
            return remote(src.at[hop, q, part], dst.at[hop, q, part], send.at[hop, q, slot],
                          recv.at[hop, q, slot], {"row": row, "col": col_at(peer, core)})

        stage2 = (send2, recv2, s2_send, s2_recv)
        stage3 = (send3, recv3, s3_send, s3_recv)

        def stage_a(q, copy):
            copy.wait()
            sent = []
            if q in Z_FIRST:
                for dx in range(4):
                    for t in range(CHUNK):
                        send2[hop, q, 4 + dx, t] = value(q, 4 + dx, t).astype(jnp.bfloat16)
                sent.append(along(stage2, q, pl.ds(4, 4), 0, 4))
                keep = range(4)
            else:
                for dx in (2, 1, 3):
                    for dz in range(2):
                        for t in range(CHUNK):
                            send2[hop, q, 2 * dx + dz, t] = value(
                                q, 4 * dz + dx, t).astype(jnp.bfloat16)
                    sent.append(along(stage2, q, pl.ds(2 * dx, 2), dx, dx))
                keep = (0, 4)
            for n, j in enumerate(keep):
                for t in range(CHUNK):
                    own[q, n, t] = value(q, j, t)
            return sent

        def stage_b(q, copies):
            for copy in copies:
                copy.wait()
            sent = []
            if q in Z_FIRST:
                for dx in (2, 1, 3):
                    for t in range(CHUNK):
                        total = own[q, dx, t] + recv2[hop, q, 4 + dx, t].astype(jnp.float32)
                        send3[hop, q, dx, t] = total.astype(jnp.bfloat16)
                    sent.append(along(stage3, q, dx, dx, dx))
                return sent
            for t in range(CHUNK):
                total = own[q, 1, t]
                for dx in range(1, 4):
                    total = total + recv2[hop, q, 2 * dx + 1, t].astype(jnp.float32)
                send3[hop, q, 0, t] = total.astype(jnp.bfloat16)
            sent.append(along(stage3, q, 0, 0, 4))
            return sent

        def reduce(q, sent):
            for copy in sent:
                copy.wait()
            for t in range(CHUNK):
                total = own[q, 0, t]
                if q in Z_FIRST:
                    total = total + recv2[hop, q, 4, t].astype(jnp.float32)
                    for dx in range(1, 4):
                        total = total + recv3[hop, q, dx, t].astype(jnp.float32)
                else:
                    for dx in range(1, 4):
                        total = total + recv2[hop, q, 2 * dx, t].astype(jnp.float32)
                    total = total + recv3[hop, q, 0, t].astype(jnp.float32)
                at = q * CHUNK + t
                gathered[hop + 1][row * PIECE + at] = (
                    scale2_ref[at] * total
                ).astype(jnp.bfloat16)
            return gather_start(hop + 1, q)

        first, second, third, copies, forwards = {}, {}, {}, {}, {}
        for name, q in SCHEDULE:
            if name == "f":
                first[q] = fill(q)
            elif name == "a":
                second[q] = stage_a(q, first[q])
            elif name == "b":
                third[q] = stage_b(q, second[q])
            elif name == "r":
                copies[q] = reduce(q, third[q])
            else:
                forwards[q] = gather_forward(hop + 1, q, copies[q])

    def dense(r, _):
        block[pl.ds(pl.multiple_of(r * TILE, TILE), TILE), :] = sums[table_smem[5, r]]
        return 0

    lax.fori_loop(0, ROW_TILES, dense, 0)

    def pick(c):
        def some(i, _):
            for u in range(16):
                n = i * 16 + u
                rows_tmp[pl.ds(n, 1), :] = block[pl.ds(rows_smem[c, 0, n], 1), :]
            return 0

        lax.fori_loop(0, NEW // 16, some, 0)
        return rows_tmp[...]

    first = []
    for j in ORDER + (0,):
        pick1[j] = pick(col_at(j, 1 - core)).astype(jnp.bfloat16)
        first.append(remote(pick1.at[j], pickr1.at[j], p1_send.at[j], p1_recv.at[j], sibling))
    second = []
    for copy, j in zip(first, ORDER + (0,)):
        mine = pick(col_at(j, core))
        copy.wait()
        value = mine + pickr1[j].astype(jnp.float32)
        if j == 0:
            out_ref[...] = value
        else:
            pick2[j] = value.astype(jnp.bfloat16)
            second.append(
                remote(pick2.at[j], pickr2.at[j], p2_send.at[j], p2_recv.at[j],
                       {"row": row, "col": col_at(j, core)})
            )
    for copy in second:
        copy.wait()
    total = out_ref[...]
    for j in range(1, 8):
        total = total + pickr2[j].astype(jnp.float32)
    square = jnp.sum(total * total, axis=1, keepdims=True)
    out_ref[...] = target[...] * total * lax.rsqrt(square + 1e-06)


def local(
    embed, degree, tile_row, tile_col, tile_count, tile_values, new_rows, new_bucket, bucket_norm
):
    smem = pl.BlockSpec(memory_space=pltpu.SMEM)
    vmem = pl.BlockSpec(memory_space=pltpu.VMEM)
    bf16, f32 = jnp.bfloat16, jnp.float32
    dma = pltpu.SemaphoreType.DMA
    return pl.pallas_call(
        kernel,
        name="propagate",
        out_shape=jax.ShapeDtypeStruct((NEW, TILE), f32),
        in_specs=[smem] * 2 + [vmem] * 6 + [pl.BlockSpec(memory_space=pl.ANY)],
        out_specs=vmem,
        scratch_shapes=[
            pltpu.VMEM((8, SLOTS), jnp.int32),
            pltpu.SMEM((8, SLOTS), jnp.int32),
            pltpu.VMEM((PIECE, TILE, TILE), f32),
            pltpu.VMEM((NEW, TILE), f32),
            pltpu.VMEM((SLOTS + 1, TILE, TILE), bf16),
            pltpu.VMEM((32, TILE, TILE), bf16),
            pltpu.VMEM((32, TILE, TILE), bf16),
            pltpu.VMEM((32, TILE, TILE), bf16),
            pltpu.VMEM((PAIRS + 1, TILE, TILE), f32),
            pltpu.VMEM((ROW_TILES * TILE, TILE), f32),
            pltpu.VMEM((2, CHUNKS, 8, CHUNK, TILE, TILE), bf16),
            pltpu.VMEM((2, CHUNKS, 8, CHUNK, TILE, TILE), bf16),
            pltpu.VMEM((2, CHUNKS, 8, CHUNK, TILE, TILE), bf16),
            pltpu.VMEM((2, CHUNKS, 8, CHUNK, TILE, TILE), bf16),
            pltpu.VMEM((2, CHUNKS, 4, CHUNK, TILE, TILE), bf16),
            pltpu.VMEM((2, CHUNKS, 4, CHUNK, TILE, TILE), bf16),
            pltpu.VMEM((CHUNKS, 4, CHUNK, TILE, TILE), f32),
            pltpu.VMEM((16, 1, NEW), jnp.int32),
            pltpu.SMEM((16, 1, NEW), jnp.int32),
            pltpu.VMEM((NEW, TILE), f32),
            pltpu.VMEM((8, NEW, TILE), bf16),
            pltpu.VMEM((8, NEW, TILE), bf16),
            pltpu.VMEM((8, NEW, TILE), bf16),
            pltpu.VMEM((8, NEW, TILE), bf16),
            dma, dma, dma,
            dma((HOPS, CHUNKS, 7)), dma((HOPS, CHUNKS, 7)), dma((2, CHUNKS)), dma((2, CHUNKS)),
            dma((2, CHUNKS, 4)), dma((2, CHUNKS, 4)), dma((2, CHUNKS, 4)), dma((2, CHUNKS, 4)), dma((16,)), dma((16,)),
            dma((8,)), dma((8,)), dma((8,)), dma((8,)),
        ],
        compiler_params=pltpu.CompilerParams(
            collective_id=0, has_side_effects=True, vmem_limit_bytes=56 << 20
        ),
    )(
        tile_count, bucket_norm, embed.reshape(PIECE, TILE, TILE), degree.reshape(PIECE, TILE),
        tile_row[0], tile_col[0], new_rows.reshape(1, NEW), new_bucket.reshape(NEW // TILE, TILE),
        tile_values[0, 0],
    )


def solution(mesh):
    in_specs = (
        P(("row", "col"), None),
        P(("row", "col")),
        P("row", "col", None),
        P("row", "col", None),
        P("row", "col"),
        P("row", "col", None, None, None),
        P(("row", "col")),
        P(("row", "col")),
        P(),
    )
    out_specs = P(("row", "col"), None)
    return jax.shard_map(local, mesh=mesh, in_specs=in_specs, out_specs=out_specs, check_vma=False)
```

```python
import functools

import jax
import jax.numpy as jnp
from jax import lax
from jax.experimental import pallas as pl
from jax.experimental.pallas import tpu as pltpu
from jax.sharding import PartitionSpec as P

HOPS = 3
TILE = 128
ROW_TILES = 64
PIECE = 4
SLOTS = 256
PAIRS = 160
NEW = 256
UNROLL = 32
CHUNKS = 2
CHUNK = PIECE // CHUNKS
Z_FIRST = (1,)
Y_FIRST = (0,)
DIRECT = ()
ORDER = (6, 5, 7, 4, 2, 1, 3)
SCHEDULE = tuple(
    (step[0], int(step[1])) for step in "f0 f1 a0 a1 b0 b1 r0 r1 g0 g1".split()
)
MESH = pl.DeviceIdType.MESH


def kernel(
    count_ref, norm_ref, embed_ref, degree_ref, trow_ref, tcol_ref, rows_ref, bucket_ref, tiles_ref,
    out_ref,
    table, table_smem, scale2_ref, target,
    tiles, state0, state1, state2, sums, block, send1, recv1, send2, recv2, send3, recv3, own, rows_all, rows_smem, rows_tmp,
    pick1, pickr1, pick2, pickr2,
    tiles_sem, rows_sem, table_sem, ag_send, ag_recv, s1_send, s1_recv, s2_send, s2_recv, s3_send, s3_recv, nr_send, nr_recv,
    p1_send, p1_recv, p2_send, p2_recv,
):
    gathered = (state0, state1, state2)
    row = lax.axis_index("row")
    col = lax.axis_index("col")
    z_lo = col // 8
    x = (col // 2) % 4
    core = col % 2

    load = pltpu.make_async_copy(tiles_ref, tiles.at[pl.ds(0, SLOTS)], tiles_sem)
    load.start()

    def row_peer(j):
        z_hi = (row // 4 + j // 4) % 2
        y = (row % 4 + j % 4) % 4
        return {"row": z_hi * 4 + y, "col": col}

    def col_at(j, k):
        return ((z_lo + j // 4) % 2) * 8 + ((x + j % 4) % 4) * 2 + k

    sibling = {"row": row, "col": col + 1 - 2 * core}

    barrier = pltpu.get_barrier_semaphore()
    for j in range(1, 8):
        pl.semaphore_signal(barrier, inc=1, device_id=row_peer(j), device_id_type=MESH)
    for j in range(1, 16):
        peer = {"row": row, "col": (col + j) % 16}
        pl.semaphore_signal(barrier, inc=1, device_id=peer, device_id_type=MESH)

    def column(values, width=None):
        n = values.shape[1]
        return jnp.transpose(jnp.broadcast_to(values, (width or n, n)))

    scale = lax.rsqrt(degree_ref[...].astype(jnp.float32))
    for t in range(PIECE):
        wide = column(scale[t : t + 1], TILE)
        state0[row * PIECE + t] = (wide * embed_ref[t].astype(jnp.float32)).astype(jnp.bfloat16)
        scale2_ref[t] = wide * wide
    tiles[SLOTS] = jnp.zeros((TILE, TILE), jnp.bfloat16)
    sums[PAIRS] = jnp.zeros((TILE, TILE), jnp.float32)
    rows_all[col] = jnp.clip(
        rows_ref[...] - row * (ROW_TILES * TILE), 0, ROW_TILES * TILE - 1
    )
    pl.semaphore_wait(barrier, 22)

    def remote(src, dst, send, recv, peer):
        copy = pltpu.make_async_remote_copy(
            src_ref=src, dst_ref=dst, send_sem=send, recv_sem=recv,
            device_id=peer, device_id_type=MESH,
        )
        copy.start()
        return copy

    def chunk(hop, who, q):
        return gathered[hop].at[pl.ds(who * PIECE + q * CHUNK, CHUNK)]

    def gather_start(hop, q):
        mine = chunk(hop, row, q)
        return [
            remote(mine, mine, ag_send.at[hop, q, j], ag_recv.at[hop, q, j], row_peer(peer))
            for j, peer in enumerate((4, 2, 1, 3) + ((6, 5, 7) if hop in DIRECT else ()))
        ]

    def gather_forward(hop, q, copies):
        sent = []
        if hop in DIRECT:
            return sent
        if q not in Y_FIRST:
            copies[0].wait_recv()
        for j, dy in ((1, 2), (2, 1), (3, 3)):
            if q in Y_FIRST:
                copies[j].wait_recv()
                theirs = chunk(hop, (row // 4) * 4 + (row + 4 - dy) % 4, q)
            else:
                theirs = chunk(hop, (row + 4) % 8, q)
            peer = row_peer(4 if q in Y_FIRST else dy)
            sent.append(remote(theirs, theirs, ag_send.at[hop, q, 3 + j],
                               ag_recv.at[hop, q, 3 + j], peer))
        return sent

    def gather_end(hop, copies, forwards):
        for q in range(CHUNKS):
            for j, copy in enumerate(copies[q]):
                copy.wait_send()
                if hop in DIRECT or (j == 0) == (q in Y_FIRST):
                    copy.wait_recv()
            for copy in forwards[q]:
                copy.wait()

    row_copies = [
        remote(
            rows_all.at[col], rows_all.at[col], nr_send.at[j], nr_recv.at[j],
            {"row": row, "col": (col + j) % 16},
        )
        for j in range(1, 16)
    ]
    copies = [gather_start(0, q) for q in range(CHUNKS)]

    ids = lax.broadcasted_iota(jnp.int32, (1, SLOTS), 1)
    live = ids < count_ref[0, 0]
    key = jnp.where(live, trow_ref[...], ROW_TILES)
    sub = lax.broadcasted_iota(jnp.int32, (SLOTS, SLOTS), 0)
    lane = lax.broadcasted_iota(jnp.int32, (SLOTS, SLOTS), 1)

    def count(mask):
        return jnp.sum(jnp.where(mask, 1, 0), axis=0, keepdims=True)

    before = count((column(key) == key) & (sub < lane))
    opener = column(jnp.where(before % 2 == 0, key, ROW_TILES))
    place_row = jnp.where(live, 2 * count(opener < key) + before, 4 * SLOTS)
    place = column(place_row)
    source = column(tcol_ref[...])

    def total_of(mask, values):
        return jnp.sum(jnp.where(mask, values, 0), axis=0, keepdims=True)

    for half in range(2):
        hit = place == 2 * lane + half
        table[half : half + 1, :] = jnp.clip(total_of(hit, sub - SLOTS) + SLOTS, 0, SLOTS)
        table[half + 2 : half + 3, :] = jnp.clip(total_of(hit, source), 0, 31)
    starts = column(jnp.where(before == 0, place_row, 4 * SLOTS))
    table[4:5, :] = 1 - count(starts == 2 * lane)
    upto = count(opener <= lane)
    table[5:6, :] = jnp.clip(
        jnp.where(count(opener == lane) > 0, upto - 1, PAIRS), 0, PAIRS
    )
    to_table = pltpu.make_async_copy(table, table_smem, table_sem)
    to_table.start()

    forwards = [gather_forward(0, q, copies[q]) for q in range(CHUNKS)]
    for t in range(NEW // TILE):
        chosen = jnp.zeros((1, TILE), jnp.float32)
        for b in range(16):
            chosen = jnp.where(bucket_ref[t : t + 1] == b, norm_ref[b], chosen)
        target[t * TILE : (t + 1) * TILE] = column(chosen, TILE)
    load.wait()
    to_table.wait()
    for copy in row_copies:
        copy.wait()
    to_smem = pltpu.make_async_copy(rows_all, rows_smem, rows_sem)
    to_smem.start()
    to_smem.wait()

    for hop in range(HOPS):
        gather_end(hop, copies, forwards)
        state = gathered[hop]

        def step(i, acc):
            for u in range(UNROLL):
                p = i * UNROLL + u
                lhs = jnp.concatenate([tiles[table_smem[0, p]], tiles[table_smem[1, p]]], axis=1)
                rhs = jnp.concatenate([state[table_smem[2, p]], state[table_smem[3, p]]], axis=0)
                prod = jnp.dot(lhs, rhs, preferred_element_type=jnp.float32)
                acc = prod + jnp.where(table_smem[4, p] > 0, acc, jnp.float32(0.0))
                sums[p] = acc
            return acc

        lax.fori_loop(0, PAIRS // UNROLL, step, jnp.zeros((TILE, TILE), jnp.float32))
        if hop == HOPS - 1:
            break

        def mine(j, k, q, t):
            return sums[table_smem[5, col_at(j, k) * PIECE + q * CHUNK + t]]

        def fill(q):
            for j in range(8):
                for t in range(CHUNK):
                    send1[hop, q, j, t] = mine(j, 1 - core, q, t).astype(jnp.bfloat16)
            return remote(send1.at[hop, q], recv1.at[hop, q], s1_send.at[hop, q],
                          s1_recv.at[hop, q], sibling)

        def value(q, j, t):
            return mine(j, core, q, t) + recv1[hop, q, j, t].astype(jnp.float32)

        def along(kind, q, part, slot, peer):
            src, dst, send, recv = kind
            return remote(src.at[hop, q, part], dst.at[hop, q, part], send.at[hop, q, slot],
                          recv.at[hop, q, slot], {"row": row, "col": col_at(peer, core)})

        stage2 = (send2, recv2, s2_send, s2_recv)
        stage3 = (send3, recv3, s3_send, s3_recv)

        def stage_a(q, copy):
            copy.wait()
            sent = []
            if q in Z_FIRST:
                for dx in range(4):
                    for t in range(CHUNK):
                        send2[hop, q, 4 + dx, t] = value(q, 4 + dx, t).astype(jnp.bfloat16)
                sent.append(along(stage2, q, pl.ds(4, 4), 0, 4))
                keep = range(4)
            else:
                for dx in (2, 1, 3):
                    for dz in range(2):
                        for t in range(CHUNK):
                            send2[hop, q, 2 * dx + dz, t] = value(
                                q, 4 * dz + dx, t).astype(jnp.bfloat16)
                    sent.append(along(stage2, q, pl.ds(2 * dx, 2), dx, dx))
                keep = (0, 4)
            for n, j in enumerate(keep):
                for t in range(CHUNK):
                    own[q, n, t] = value(q, j, t)
            return sent

        def stage_b(q, copies):
            for copy in copies:
                copy.wait()
            sent = []
            if q in Z_FIRST:
                for dx in (2, 1, 3):
                    for t in range(CHUNK):
                        total = own[q, dx, t] + recv2[hop, q, 4 + dx, t].astype(jnp.float32)
                        send3[hop, q, dx, t] = total.astype(jnp.bfloat16)
                    sent.append(along(stage3, q, dx, dx, dx))
                return sent
            for t in range(CHUNK):
                total = own[q, 1, t]
                for dx in range(1, 4):
                    total = total + recv2[hop, q, 2 * dx + 1, t].astype(jnp.float32)
                send3[hop, q, 0, t] = total.astype(jnp.bfloat16)
            sent.append(along(stage3, q, 0, 0, 4))
            return sent

        def reduce(q, sent):
            for copy in sent:
                copy.wait()
            for t in range(CHUNK):
                total = own[q, 0, t]
                if q in Z_FIRST:
                    total = total + recv2[hop, q, 4, t].astype(jnp.float32)
                    for dx in range(1, 4):
                        total = total + recv3[hop, q, dx, t].astype(jnp.float32)
                else:
                    for dx in range(1, 4):
                        total = total + recv2[hop, q, 2 * dx, t].astype(jnp.float32)
                    total = total + recv3[hop, q, 0, t].astype(jnp.float32)
                at = q * CHUNK + t
                gathered[hop + 1][row * PIECE + at] = (
                    scale2_ref[at] * total
                ).astype(jnp.bfloat16)
            return gather_start(hop + 1, q)

        first, second, third, copies, forwards = {}, {}, {}, {}, {}
        for name, q in SCHEDULE:
            if name == "f":
                first[q] = fill(q)
            elif name == "a":
                second[q] = stage_a(q, first[q])
            elif name == "b":
                third[q] = stage_b(q, second[q])
            elif name == "r":
                copies[q] = reduce(q, third[q])
            else:
                forwards[q] = gather_forward(hop + 1, q, copies[q])

    def dense(r, _):
        block[pl.ds(pl.multiple_of(r * TILE, TILE), TILE), :] = sums[table_smem[5, r]]
        return 0

    lax.fori_loop(0, ROW_TILES, dense, 0)

    def pick(c):
        def some(i, _):
            for u in range(16):
                n = i * 16 + u
                rows_tmp[pl.ds(n, 1), :] = block[pl.ds(rows_smem[c, 0, n], 1), :]
            return 0

        lax.fori_loop(0, NEW // 16, some, 0)
        return rows_tmp[...]

    first = []
    for j in ORDER + (0,):
        pick1[j] = pick(col_at(j, 1 - core)).astype(jnp.bfloat16)
        first.append(remote(pick1.at[j], pickr1.at[j], p1_send.at[j], p1_recv.at[j], sibling))
    second = []
    for copy, j in zip(first, ORDER + (0,)):
        mine = pick(col_at(j, core))
        copy.wait()
        value = mine + pickr1[j].astype(jnp.float32)
        if j == 0:
            out_ref[...] = value
        else:
            pick2[j] = value.astype(jnp.bfloat16)
            second.append(
                remote(pick2.at[j], pickr2.at[j], p2_send.at[j], p2_recv.at[j],
                       {"row": row, "col": col_at(j, core)})
            )
    for copy in second:
        copy.wait()
    total = out_ref[...]
    for j in range(1, 8):
        total = total + pickr2[j].astype(jnp.float32)
    square = jnp.sum(total * total, axis=1, keepdims=True)
    out_ref[...] = target[...] * total * lax.rsqrt(square + 1e-06)


def local(
    embed, degree, tile_row, tile_col, tile_count, tile_values, new_rows, new_bucket, bucket_norm
):
    smem = pl.BlockSpec(memory_space=pltpu.SMEM)
    vmem = pl.BlockSpec(memory_space=pltpu.VMEM)
    bf16, f32 = jnp.bfloat16, jnp.float32
    dma = pltpu.SemaphoreType.DMA
    return pl.pallas_call(
        kernel,
        name="propagate",
        out_shape=jax.ShapeDtypeStruct((NEW, TILE), f32),
        in_specs=[smem] * 2 + [vmem] * 6 + [pl.BlockSpec(memory_space=pl.ANY)],
        out_specs=vmem,
        scratch_shapes=[
            pltpu.VMEM((8, SLOTS), jnp.int32),
            pltpu.SMEM((8, SLOTS), jnp.int32),
            pltpu.VMEM((PIECE, TILE, TILE), f32),
            pltpu.VMEM((NEW, TILE), f32),
            pltpu.VMEM((SLOTS + 1, TILE, TILE), bf16),
            pltpu.VMEM((32, TILE, TILE), bf16),
            pltpu.VMEM((32, TILE, TILE), bf16),
            pltpu.VMEM((32, TILE, TILE), bf16),
            pltpu.VMEM((PAIRS + 1, TILE, TILE), f32),
            pltpu.VMEM((ROW_TILES * TILE, TILE), f32),
            pltpu.VMEM((2, CHUNKS, 8, CHUNK, TILE, TILE), bf16),
            pltpu.VMEM((2, CHUNKS, 8, CHUNK, TILE, TILE), bf16),
            pltpu.VMEM((2, CHUNKS, 8, CHUNK, TILE, TILE), bf16),
            pltpu.VMEM((2, CHUNKS, 8, CHUNK, TILE, TILE), bf16),
            pltpu.VMEM((2, CHUNKS, 4, CHUNK, TILE, TILE), bf16),
            pltpu.VMEM((2, CHUNKS, 4, CHUNK, TILE, TILE), bf16),
            pltpu.VMEM((CHUNKS, 4, CHUNK, TILE, TILE), f32),
            pltpu.VMEM((16, 1, NEW), jnp.int32),
            pltpu.SMEM((16, 1, NEW), jnp.int32),
            pltpu.VMEM((NEW, TILE), f32),
            pltpu.VMEM((8, NEW, TILE), bf16),
            pltpu.VMEM((8, NEW, TILE), bf16),
            pltpu.VMEM((8, NEW, TILE), bf16),
            pltpu.VMEM((8, NEW, TILE), bf16),
            dma, dma, dma,
            dma((HOPS, CHUNKS, 7)), dma((HOPS, CHUNKS, 7)), dma((2, CHUNKS)), dma((2, CHUNKS)),
            dma((2, CHUNKS, 4)), dma((2, CHUNKS, 4)), dma((2, CHUNKS, 4)), dma((2, CHUNKS, 4)), dma((16,)), dma((16,)),
            dma((8,)), dma((8,)), dma((8,)), dma((8,)),
        ],
        compiler_params=pltpu.CompilerParams(
            collective_id=0, has_side_effects=True, vmem_limit_bytes=56 << 20
        ),
    )(
        tile_count, bucket_norm, embed.reshape(PIECE, TILE, TILE), degree.reshape(PIECE, TILE),
        tile_row[0], tile_col[0], new_rows.reshape(1, NEW), new_bucket.reshape(NEW // TILE, TILE),
        tile_values[0, 0],
    )


def solution(mesh):
    in_specs = (
        P(("row", "col"), None),
        P(("row", "col")),
        P("row", "col", None),
        P("row", "col", None),
        P("row", "col"),
        P("row", "col", None, None, None),
        P(("row", "col")),
        P(("row", "col")),
        P(),
    )
    out_specs = P(("row", "col"), None)
    return jax.shard_map(local, mesh=mesh, in_specs=in_specs, out_specs=out_specs, check_vma=False)
```

```python
import functools

import jax
import jax.numpy as jnp
from jax import lax
from jax.experimental import pallas as pl
from jax.experimental.pallas import tpu as pltpu
from jax.sharding import PartitionSpec as P

HOPS = 3
TILE = 128
ROW_TILES = 64
PIECE = 4
SLOTS = 256
PAIRS = 160
NEW = 256
UNROLL = 40
CHUNKS = 2
CHUNK = PIECE // CHUNKS
Z_FIRST = (1,)
Y_FIRST = (0,)
DIRECT = ()
ORDER = (6, 5, 7, 4, 2, 1, 3)
SCHEDULE = tuple(
    (step[0], int(step[1])) for step in "f0 f1 a0 a1 b0 b1 r0 r1 g0 g1".split()
)
MESH = pl.DeviceIdType.MESH


def kernel(
    count_ref, norm_ref, embed_ref, degree_ref, trow_ref, tcol_ref, rows_ref, bucket_ref, tiles_ref,
    out_ref,
    table, table_smem, scale2_ref, target,
    tiles, state0, state1, state2, sums, block, send1, recv1, send2, recv2, send3, recv3, own, rows_all, rows_smem, rows_tmp,
    pick1, pickr1, pick2, pickr2,
    tiles_sem, rows_sem, table_sem, ag_send, ag_recv, s1_send, s1_recv, s2_send, s2_recv, s3_send, s3_recv, nr_send, nr_recv,
    p1_send, p1_recv, p2_send, p2_recv,
):
    gathered = (state0, state1, state2)
    row = lax.axis_index("row")
    col = lax.axis_index("col")
    z_lo = col // 8
    x = (col // 2) % 4
    core = col % 2

    load = pltpu.make_async_copy(tiles_ref, tiles.at[pl.ds(0, SLOTS)], tiles_sem)
    load.start()

    def row_peer(j):
        z_hi = (row // 4 + j // 4) % 2
        y = (row % 4 + j % 4) % 4
        return {"row": z_hi * 4 + y, "col": col}

    def col_at(j, k):
        return ((z_lo + j // 4) % 2) * 8 + ((x + j % 4) % 4) * 2 + k

    sibling = {"row": row, "col": col + 1 - 2 * core}

    barrier = pltpu.get_barrier_semaphore()
    for j in range(1, 8):
        pl.semaphore_signal(barrier, inc=1, device_id=row_peer(j), device_id_type=MESH)
    for j in range(1, 16):
        peer = {"row": row, "col": (col + j) % 16}
        pl.semaphore_signal(barrier, inc=1, device_id=peer, device_id_type=MESH)

    def column(values, width=None):
        n = values.shape[1]
        return jnp.transpose(jnp.broadcast_to(values, (width or n, n)))

    scale = lax.rsqrt(degree_ref[...].astype(jnp.float32))
    for t in range(PIECE):
        wide = column(scale[t : t + 1], TILE)
        state0[row * PIECE + t] = (wide * embed_ref[t].astype(jnp.float32)).astype(jnp.bfloat16)
        scale2_ref[t] = wide * wide
    tiles[SLOTS] = jnp.zeros((TILE, TILE), jnp.bfloat16)
    sums[PAIRS] = jnp.zeros((TILE, TILE), jnp.float32)
    rows_all[col] = jnp.clip(
        rows_ref[...] - row * (ROW_TILES * TILE), 0, ROW_TILES * TILE - 1
    )
    pl.semaphore_wait(barrier, 22)

    def remote(src, dst, send, recv, peer):
        copy = pltpu.make_async_remote_copy(
            src_ref=src, dst_ref=dst, send_sem=send, recv_sem=recv,
            device_id=peer, device_id_type=MESH,
        )
        copy.start()
        return copy

    def chunk(hop, who, q):
        return gathered[hop].at[pl.ds(who * PIECE + q * CHUNK, CHUNK)]

    def gather_start(hop, q):
        mine = chunk(hop, row, q)
        return [
            remote(mine, mine, ag_send.at[hop, q, j], ag_recv.at[hop, q, j], row_peer(peer))
            for j, peer in enumerate((4, 2, 1, 3) + ((6, 5, 7) if hop in DIRECT else ()))
        ]

    def gather_forward(hop, q, copies):
        sent = []
        if hop in DIRECT:
            return sent
        if q not in Y_FIRST:
            copies[0].wait_recv()
        for j, dy in ((1, 2), (2, 1), (3, 3)):
            if q in Y_FIRST:
                copies[j].wait_recv()
                theirs = chunk(hop, (row // 4) * 4 + (row + 4 - dy) % 4, q)
            else:
                theirs = chunk(hop, (row + 4) % 8, q)
            peer = row_peer(4 if q in Y_FIRST else dy)
            sent.append(remote(theirs, theirs, ag_send.at[hop, q, 3 + j],
                               ag_recv.at[hop, q, 3 + j], peer))
        return sent

    def gather_end(hop, copies, forwards):
        for q in range(CHUNKS):
            for j, copy in enumerate(copies[q]):
                copy.wait_send()
                if hop in DIRECT or (j == 0) == (q in Y_FIRST):
                    copy.wait_recv()
            for copy in forwards[q]:
                copy.wait()

    row_copies = [
        remote(
            rows_all.at[col], rows_all.at[col], nr_send.at[j], nr_recv.at[j],
            {"row": row, "col": (col + j) % 16},
        )
        for j in range(1, 16)
    ]
    copies = [gather_start(0, q) for q in range(CHUNKS)]

    ids = lax.broadcasted_iota(jnp.int32, (1, SLOTS), 1)
    live = ids < count_ref[0, 0]
    key = jnp.where(live, trow_ref[...], ROW_TILES)
    sub = lax.broadcasted_iota(jnp.int32, (SLOTS, SLOTS), 0)
    lane = lax.broadcasted_iota(jnp.int32, (SLOTS, SLOTS), 1)

    def count(mask):
        return jnp.sum(jnp.where(mask, 1, 0), axis=0, keepdims=True)

    before = count((column(key) == key) & (sub < lane))
    opener = column(jnp.where(before % 2 == 0, key, ROW_TILES))
    place_row = jnp.where(live, 2 * count(opener < key) + before, 4 * SLOTS)
    place = column(place_row)
    source = column(tcol_ref[...])

    def total_of(mask, values):
        return jnp.sum(jnp.where(mask, values, 0), axis=0, keepdims=True)

    for half in range(2):
        hit = place == 2 * lane + half
        table[half : half + 1, :] = jnp.clip(total_of(hit, sub - SLOTS) + SLOTS, 0, SLOTS)
        table[half + 2 : half + 3, :] = jnp.clip(total_of(hit, source), 0, 31)
    starts = column(jnp.where(before == 0, place_row, 4 * SLOTS))
    table[4:5, :] = 1 - count(starts == 2 * lane)
    upto = count(opener <= lane)
    table[5:6, :] = jnp.clip(
        jnp.where(count(opener == lane) > 0, upto - 1, PAIRS), 0, PAIRS
    )
    to_table = pltpu.make_async_copy(table, table_smem, table_sem)
    to_table.start()

    forwards = [gather_forward(0, q, copies[q]) for q in range(CHUNKS)]
    for t in range(NEW // TILE):
        chosen = jnp.zeros((1, TILE), jnp.float32)
        for b in range(16):
            chosen = jnp.where(bucket_ref[t : t + 1] == b, norm_ref[b], chosen)
        target[t * TILE : (t + 1) * TILE] = column(chosen, TILE)
    load.wait()
    to_table.wait()
    for copy in row_copies:
        copy.wait()
    to_smem = pltpu.make_async_copy(rows_all, rows_smem, rows_sem)
    to_smem.start()
    to_smem.wait()

    for hop in range(HOPS):
        gather_end(hop, copies, forwards)
        state = gathered[hop]

        def step(i, acc):
            for u in range(UNROLL):
                p = i * UNROLL + u
                lhs = jnp.concatenate([tiles[table_smem[0, p]], tiles[table_smem[1, p]]], axis=1)
                rhs = jnp.concatenate([state[table_smem[2, p]], state[table_smem[3, p]]], axis=0)
                prod = jnp.dot(lhs, rhs, preferred_element_type=jnp.float32)
                acc = prod + jnp.where(table_smem[4, p] > 0, acc, jnp.float32(0.0))
                sums[p] = acc
            return acc

        lax.fori_loop(0, PAIRS // UNROLL, step, jnp.zeros((TILE, TILE), jnp.float32))
        if hop == HOPS - 1:
            break

        def mine(j, k, q, t):
            return sums[table_smem[5, col_at(j, k) * PIECE + q * CHUNK + t]]

        def fill(q):
            for j in range(8):
                for t in range(CHUNK):
                    send1[hop, q, j, t] = mine(j, 1 - core, q, t).astype(jnp.bfloat16)
            return remote(send1.at[hop, q], recv1.at[hop, q], s1_send.at[hop, q],
                          s1_recv.at[hop, q], sibling)

        def value(q, j, t):
            return mine(j, core, q, t) + recv1[hop, q, j, t].astype(jnp.float32)

        def along(kind, q, part, slot, peer):
            src, dst, send, recv = kind
            return remote(src.at[hop, q, part], dst.at[hop, q, part], send.at[hop, q, slot],
                          recv.at[hop, q, slot], {"row": row, "col": col_at(peer, core)})

        stage2 = (send2, recv2, s2_send, s2_recv)
        stage3 = (send3, recv3, s3_send, s3_recv)

        def stage_a(q, copy):
            copy.wait()
            sent = []
            if q in Z_FIRST:
                for dx in range(4):
                    for t in range(CHUNK):
                        send2[hop, q, 4 + dx, t] = value(q, 4 + dx, t).astype(jnp.bfloat16)
                sent.append(along(stage2, q, pl.ds(4, 4), 0, 4))
                keep = range(4)
            else:
                for dx in (2, 1, 3):
                    for dz in range(2):
                        for t in range(CHUNK):
                            send2[hop, q, 2 * dx + dz, t] = value(
                                q, 4 * dz + dx, t).astype(jnp.bfloat16)
                    sent.append(along(stage2, q, pl.ds(2 * dx, 2), dx, dx))
                keep = (0, 4)
            for n, j in enumerate(keep):
                for t in range(CHUNK):
                    own[q, n, t] = value(q, j, t)
            return sent

        def stage_b(q, copies):
            for copy in copies:
                copy.wait()
            sent = []
            if q in Z_FIRST:
                for dx in (2, 1, 3):
                    for t in range(CHUNK):
                        total = own[q, dx, t] + recv2[hop, q, 4 + dx, t].astype(jnp.float32)
                        send3[hop, q, dx, t] = total.astype(jnp.bfloat16)
                    sent.append(along(stage3, q, dx, dx, dx))
                return sent
            for t in range(CHUNK):
                total = own[q, 1, t]
                for dx in range(1, 4):
                    total = total + recv2[hop, q, 2 * dx + 1, t].astype(jnp.float32)
                send3[hop, q, 0, t] = total.astype(jnp.bfloat16)
            sent.append(along(stage3, q, 0, 0, 4))
            return sent

        def reduce(q, sent):
            for copy in sent:
                copy.wait()
            for t in range(CHUNK):
                total = own[q, 0, t]
                if q in Z_FIRST:
                    total = total + recv2[hop, q, 4, t].astype(jnp.float32)
                    for dx in range(1, 4):
                        total = total + recv3[hop, q, dx, t].astype(jnp.float32)
                else:
                    for dx in range(1, 4):
                        total = total + recv2[hop, q, 2 * dx, t].astype(jnp.float32)
                    total = total + recv3[hop, q, 0, t].astype(jnp.float32)
                at = q * CHUNK + t
                gathered[hop + 1][row * PIECE + at] = (
                    scale2_ref[at] * total
                ).astype(jnp.bfloat16)
            return gather_start(hop + 1, q)

        first, second, third, copies, forwards = {}, {}, {}, {}, {}
        for name, q in SCHEDULE:
            if name == "f":
                first[q] = fill(q)
            elif name == "a":
                second[q] = stage_a(q, first[q])
            elif name == "b":
                third[q] = stage_b(q, second[q])
            elif name == "r":
                copies[q] = reduce(q, third[q])
            else:
                forwards[q] = gather_forward(hop + 1, q, copies[q])

    def dense(r, _):
        for u in range(8):
            at = pl.multiple_of((r * 8 + u) * TILE, TILE)
            block[pl.ds(at, TILE), :] = sums[table_smem[5, r * 8 + u]]
        return 0

    lax.fori_loop(0, ROW_TILES // 8, dense, 0)

    def pick(c):
        def some(i, _):
            for u in range(16):
                n = i * 16 + u
                rows_tmp[pl.ds(n, 1), :] = block[pl.ds(rows_smem[c, 0, n], 1), :]
            return 0

        lax.fori_loop(0, NEW // 16, some, 0)
        return rows_tmp[...]

    first = []
    for j in ORDER + (0,):
        pick1[j] = pick(col_at(j, 1 - core)).astype(jnp.bfloat16)
        first.append(remote(pick1.at[j], pickr1.at[j], p1_send.at[j], p1_recv.at[j], sibling))
    second = []
    for copy, j in zip(first, ORDER + (0,)):
        mine = pick(col_at(j, core))
        copy.wait()
        value = mine + pickr1[j].astype(jnp.float32)
        if j == 0:
            out_ref[...] = value
        else:
            pick2[j] = value.astype(jnp.bfloat16)
            second.append(
                remote(pick2.at[j], pickr2.at[j], p2_send.at[j], p2_recv.at[j],
                       {"row": row, "col": col_at(j, core)})
            )
    for copy in second:
        copy.wait()
    total = out_ref[...]
    for j in range(1, 8):
        total = total + pickr2[j].astype(jnp.float32)
    square = jnp.sum(total * total, axis=1, keepdims=True)
    out_ref[...] = target[...] * total * lax.rsqrt(square + 1e-06)


def local(
    embed, degree, tile_row, tile_col, tile_count, tile_values, new_rows, new_bucket, bucket_norm
):
    smem = pl.BlockSpec(memory_space=pltpu.SMEM)
    vmem = pl.BlockSpec(memory_space=pltpu.VMEM)
    bf16, f32 = jnp.bfloat16, jnp.float32
    dma = pltpu.SemaphoreType.DMA
    return pl.pallas_call(
        kernel,
        name="propagate",
        out_shape=jax.ShapeDtypeStruct((NEW, TILE), f32),
        in_specs=[smem] * 2 + [vmem] * 6 + [pl.BlockSpec(memory_space=pl.ANY)],
        out_specs=vmem,
        scratch_shapes=[
            pltpu.VMEM((8, SLOTS), jnp.int32),
            pltpu.SMEM((8, SLOTS), jnp.int32),
            pltpu.VMEM((PIECE, TILE, TILE), f32),
            pltpu.VMEM((NEW, TILE), f32),
            pltpu.VMEM((SLOTS + 1, TILE, TILE), bf16),
            pltpu.VMEM((32, TILE, TILE), bf16),
            pltpu.VMEM((32, TILE, TILE), bf16),
            pltpu.VMEM((32, TILE, TILE), bf16),
            pltpu.VMEM((PAIRS + 1, TILE, TILE), f32),
            pltpu.VMEM((ROW_TILES * TILE, TILE), f32),
            pltpu.VMEM((2, CHUNKS, 8, CHUNK, TILE, TILE), bf16),
            pltpu.VMEM((2, CHUNKS, 8, CHUNK, TILE, TILE), bf16),
            pltpu.VMEM((2, CHUNKS, 8, CHUNK, TILE, TILE), bf16),
            pltpu.VMEM((2, CHUNKS, 8, CHUNK, TILE, TILE), bf16),
            pltpu.VMEM((2, CHUNKS, 4, CHUNK, TILE, TILE), bf16),
            pltpu.VMEM((2, CHUNKS, 4, CHUNK, TILE, TILE), bf16),
            pltpu.VMEM((CHUNKS, 4, CHUNK, TILE, TILE), f32),
            pltpu.VMEM((16, 1, NEW), jnp.int32),
            pltpu.SMEM((16, 1, NEW), jnp.int32),
            pltpu.VMEM((NEW, TILE), f32),
            pltpu.VMEM((8, NEW, TILE), bf16),
            pltpu.VMEM((8, NEW, TILE), bf16),
            pltpu.VMEM((8, NEW, TILE), bf16),
            pltpu.VMEM((8, NEW, TILE), bf16),
            dma, dma, dma,
            dma((HOPS, CHUNKS, 7)), dma((HOPS, CHUNKS, 7)), dma((2, CHUNKS)), dma((2, CHUNKS)),
            dma((2, CHUNKS, 4)), dma((2, CHUNKS, 4)), dma((2, CHUNKS, 4)), dma((2, CHUNKS, 4)), dma((16,)), dma((16,)),
            dma((8,)), dma((8,)), dma((8,)), dma((8,)),
        ],
        compiler_params=pltpu.CompilerParams(
            collective_id=0, has_side_effects=True, vmem_limit_bytes=56 << 20
        ),
    )(
        tile_count, bucket_norm, embed.reshape(PIECE, TILE, TILE), degree.reshape(PIECE, TILE),
        tile_row[0], tile_col[0], new_rows.reshape(1, NEW), new_bucket.reshape(NEW // TILE, TILE),
        tile_values[0, 0],
    )


def solution(mesh):
    in_specs = (
        P(("row", "col"), None),
        P(("row", "col")),
        P("row", "col", None),
        P("row", "col", None),
        P("row", "col"),
        P("row", "col", None, None, None),
        P(("row", "col")),
        P(("row", "col")),
        P(),
    )
    out_specs = P(("row", "col"), None)
    return jax.shard_map(local, mesh=mesh, in_specs=in_specs, out_specs=out_specs, check_vma=False)
```

```python
import functools

import jax
import jax.numpy as jnp
from jax import lax
from jax.experimental import pallas as pl
from jax.experimental.pallas import tpu as pltpu
from jax.sharding import PartitionSpec as P

HOPS = 3
TILE = 128
ROW_TILES = 64
PIECE = 4
SLOTS = 256
PAIRS = 160
NEW = 256
UNROLL = 40
CHUNKS = 2
CHUNK = PIECE // CHUNKS
Z_FIRST = (1,)
Y_FIRST = (0,)
DIRECT = ()
ORDER = (6, 5, 7, 4, 2, 1, 3)
SCHEDULE = tuple(
    (step[0], int(step[1])) for step in "f0 f1 a0 a1 b0 b1 r0 r1 g0 g1".split()
)
MESH = pl.DeviceIdType.MESH


def kernel(
    count_ref, norm_ref, embed_ref, degree_ref, trow_ref, tcol_ref, rows_ref, bucket_ref, tiles_ref,
    out_ref,
    table, table_smem, scale2_ref, target,
    tiles, state0, state1, state2, sums, block, send1, recv1, send2, recv2, send3, recv3, own, rows_all, rows_smem, rows_tmp,
    pick1, pickr1, pick2, pickr2,
    tiles_sem, rows_sem, table_sem, ag_send, ag_recv, s1_send, s1_recv, s2_send, s2_recv, s3_send, s3_recv, nr_send, nr_recv,
    p1_send, p1_recv, p2_send, p2_recv,
):
    gathered = (state0, state1, state2)
    row = lax.axis_index("row")
    col = lax.axis_index("col")
    z_lo = col // 8
    x = (col // 2) % 4
    core = col % 2

    load = pltpu.make_async_copy(tiles_ref, tiles.at[pl.ds(0, SLOTS)], tiles_sem)
    load.start()

    def row_peer(j):
        z_hi = (row // 4 + j // 4) % 2
        y = (row % 4 + j % 4) % 4
        return {"row": z_hi * 4 + y, "col": col}

    def col_at(j, k):
        return ((z_lo + j // 4) % 2) * 8 + ((x + j % 4) % 4) * 2 + k

    sibling = {"row": row, "col": col + 1 - 2 * core}

    barrier = pltpu.get_barrier_semaphore()
    for j in range(1, 8):
        pl.semaphore_signal(barrier, inc=1, device_id=row_peer(j), device_id_type=MESH)
    for j in range(1, 16):
        peer = {"row": row, "col": (col + j) % 16}
        pl.semaphore_signal(barrier, inc=1, device_id=peer, device_id_type=MESH)

    def column(values, width=None):
        n = values.shape[1]
        return jnp.transpose(jnp.broadcast_to(values, (width or n, n)))

    scale = lax.rsqrt(degree_ref[...].astype(jnp.float32))
    for t in range(PIECE):
        wide = column(scale[t : t + 1], TILE)
        state0[row * PIECE + t] = (wide * embed_ref[t].astype(jnp.float32)).astype(jnp.bfloat16)
        scale2_ref[t] = wide * wide
    tiles[SLOTS] = jnp.zeros((TILE, TILE), jnp.bfloat16)
    sums[PAIRS] = jnp.zeros((TILE, TILE), jnp.float32)
    rows_all[col] = jnp.clip(
        rows_ref[...] - row * (ROW_TILES * TILE), 0, ROW_TILES * TILE - 1
    )
    pl.semaphore_wait(barrier, 22)

    def remote(src, dst, send, recv, peer):
        copy = pltpu.make_async_remote_copy(
            src_ref=src, dst_ref=dst, send_sem=send, recv_sem=recv,
            device_id=peer, device_id_type=MESH,
        )
        copy.start()
        return copy

    def chunk(hop, who, q):
        return gathered[hop].at[pl.ds(who * PIECE + q * CHUNK, CHUNK)]

    def gather_start(hop, q):
        mine = chunk(hop, row, q)
        return [
            remote(mine, mine, ag_send.at[hop, q, j], ag_recv.at[hop, q, j], row_peer(peer))
            for j, peer in enumerate((4, 2, 1, 3) + ((6, 5, 7) if hop in DIRECT else ()))
        ]

    def gather_forward(hop, q, copies):
        sent = []
        if hop in DIRECT:
            return sent
        if q not in Y_FIRST:
            copies[0].wait_recv()
        for j, dy in ((1, 2), (2, 1), (3, 3)):
            if q in Y_FIRST:
                copies[j].wait_recv()
                theirs = chunk(hop, (row // 4) * 4 + (row + 4 - dy) % 4, q)
            else:
                theirs = chunk(hop, (row + 4) % 8, q)
            peer = row_peer(4 if q in Y_FIRST else dy)
            sent.append(remote(theirs, theirs, ag_send.at[hop, q, 3 + j],
                               ag_recv.at[hop, q, 3 + j], peer))
        return sent

    def gather_end(hop, copies, forwards):
        for q in range(CHUNKS):
            for j, copy in enumerate(copies[q]):
                copy.wait_send()
                if hop in DIRECT or (j == 0) == (q in Y_FIRST):
                    copy.wait_recv()
            for copy in forwards[q]:
                copy.wait()

    copies = [gather_start(0, q) for q in range(CHUNKS)]
    row_copies = [
        remote(
            rows_all.at[col], rows_all.at[col], nr_send.at[j], nr_recv.at[j],
            {"row": row, "col": (col + j) % 16},
        )
        for j in range(1, 16)
    ]

    ids = lax.broadcasted_iota(jnp.int32, (1, SLOTS), 1)
    live = ids < count_ref[0, 0]
    key = jnp.where(live, trow_ref[...], ROW_TILES)
    sub = lax.broadcasted_iota(jnp.int32, (SLOTS, SLOTS), 0)
    lane = lax.broadcasted_iota(jnp.int32, (SLOTS, SLOTS), 1)

    def count(mask):
        return jnp.sum(jnp.where(mask, 1, 0), axis=0, keepdims=True)

    before = count((column(key) == key) & (sub < lane))
    opener = column(jnp.where(before % 2 == 0, key, ROW_TILES))
    place_row = jnp.where(live, 2 * count(opener < key) + before, 4 * SLOTS)
    place = column(place_row)
    source = column(tcol_ref[...])

    def total_of(mask, values):
        return jnp.sum(jnp.where(mask, values, 0), axis=0, keepdims=True)

    for half in range(2):
        hit = place == 2 * lane + half
        table[half : half + 1, :] = jnp.clip(total_of(hit, sub - SLOTS) + SLOTS, 0, SLOTS)
        table[half + 2 : half + 3, :] = jnp.clip(total_of(hit, source), 0, 31)
    starts = column(jnp.where(before == 0, place_row, 4 * SLOTS))
    table[4:5, :] = 1 - count(starts == 2 * lane)
    upto = count(opener <= lane)
    table[5:6, :] = jnp.clip(
        jnp.where(count(opener == lane) > 0, upto - 1, PAIRS), 0, PAIRS
    )
    to_table = pltpu.make_async_copy(table, table_smem, table_sem)
    to_table.start()

    forwards = [gather_forward(0, q, copies[q]) for q in range(CHUNKS)]
    for t in range(NEW // TILE):
        chosen = jnp.zeros((1, TILE), jnp.float32)
        for b in range(16):
            chosen = jnp.where(bucket_ref[t : t + 1] == b, norm_ref[b], chosen)
        target[t * TILE : (t + 1) * TILE] = column(chosen, TILE)
    load.wait()
    to_table.wait()
    for copy in row_copies:
        copy.wait()
    to_smem = pltpu.make_async_copy(rows_all, rows_smem, rows_sem)
    to_smem.start()
    to_smem.wait()

    for hop in range(HOPS):
        gather_end(hop, copies, forwards)
        state = gathered[hop]

        def step(i, acc):
            for u in range(UNROLL):
                p = i * UNROLL + u
                lhs = jnp.concatenate([tiles[table_smem[0, p]], tiles[table_smem[1, p]]], axis=1)
                rhs = jnp.concatenate([state[table_smem[2, p]], state[table_smem[3, p]]], axis=0)
                prod = jnp.dot(lhs, rhs, preferred_element_type=jnp.float32)
                acc = prod + jnp.where(table_smem[4, p] > 0, acc, jnp.float32(0.0))
                sums[p] = acc
            return acc

        lax.fori_loop(0, PAIRS // UNROLL, step, jnp.zeros((TILE, TILE), jnp.float32))
        if hop == HOPS - 1:
            break

        def mine(j, k, q, t):
            return sums[table_smem[5, col_at(j, k) * PIECE + q * CHUNK + t]]

        def fill(q):
            for j in range(8):
                for t in range(CHUNK):
                    send1[hop, q, j, t] = mine(j, 1 - core, q, t).astype(jnp.bfloat16)
            return remote(send1.at[hop, q], recv1.at[hop, q], s1_send.at[hop, q],
                          s1_recv.at[hop, q], sibling)

        def value(q, j, t):
            return mine(j, core, q, t) + recv1[hop, q, j, t].astype(jnp.float32)

        def along(kind, q, part, slot, peer):
            src, dst, send, recv = kind
            return remote(src.at[hop, q, part], dst.at[hop, q, part], send.at[hop, q, slot],
                          recv.at[hop, q, slot], {"row": row, "col": col_at(peer, core)})

        stage2 = (send2, recv2, s2_send, s2_recv)
        stage3 = (send3, recv3, s3_send, s3_recv)

        def stage_a(q, copy):
            copy.wait()
            sent = []
            if q in Z_FIRST:
                for dx in range(4):
                    for t in range(CHUNK):
                        send2[hop, q, 4 + dx, t] = value(q, 4 + dx, t).astype(jnp.bfloat16)
                sent.append(along(stage2, q, pl.ds(4, 4), 0, 4))
                keep = range(4)
            else:
                for dx in (2, 1, 3):
                    for dz in range(2):
                        for t in range(CHUNK):
                            send2[hop, q, 2 * dx + dz, t] = value(
                                q, 4 * dz + dx, t).astype(jnp.bfloat16)
                    sent.append(along(stage2, q, pl.ds(2 * dx, 2), dx, dx))
                keep = (0, 4)
            for n, j in enumerate(keep):
                for t in range(CHUNK):
                    own[q, n, t] = value(q, j, t)
            return sent

        def stage_b(q, copies):
            for copy in copies:
                copy.wait()
            sent = []
            if q in Z_FIRST:
                for dx in (2, 1, 3):
                    for t in range(CHUNK):
                        total = own[q, dx, t] + recv2[hop, q, 4 + dx, t].astype(jnp.float32)
                        send3[hop, q, dx, t] = total.astype(jnp.bfloat16)
                    sent.append(along(stage3, q, dx, dx, dx))
                return sent
            for t in range(CHUNK):
                total = own[q, 1, t]
                for dx in range(1, 4):
                    total = total + recv2[hop, q, 2 * dx + 1, t].astype(jnp.float32)
                send3[hop, q, 0, t] = total.astype(jnp.bfloat16)
            sent.append(along(stage3, q, 0, 0, 4))
            return sent

        def reduce(q, sent):
            for copy in sent:
                copy.wait()
            for t in range(CHUNK):
                total = own[q, 0, t]
                if q in Z_FIRST:
                    total = total + recv2[hop, q, 4, t].astype(jnp.float32)
                    for dx in range(1, 4):
                        total = total + recv3[hop, q, dx, t].astype(jnp.float32)
                else:
                    for dx in range(1, 4):
                        total = total + recv2[hop, q, 2 * dx, t].astype(jnp.float32)
                    total = total + recv3[hop, q, 0, t].astype(jnp.float32)
                at = q * CHUNK + t
                gathered[hop + 1][row * PIECE + at] = (
                    scale2_ref[at] * total
                ).astype(jnp.bfloat16)
            return gather_start(hop + 1, q)

        first, second, third, copies, forwards = {}, {}, {}, {}, {}
        for name, q in SCHEDULE:
            if name == "f":
                first[q] = fill(q)
            elif name == "a":
                second[q] = stage_a(q, first[q])
            elif name == "b":
                third[q] = stage_b(q, second[q])
            elif name == "r":
                copies[q] = reduce(q, third[q])
            else:
                forwards[q] = gather_forward(hop + 1, q, copies[q])

    def dense(r, _):
        for u in range(8):
            at = pl.multiple_of((r * 8 + u) * TILE, TILE)
            block[pl.ds(at, TILE), :] = sums[table_smem[5, r * 8 + u]]
        return 0

    lax.fori_loop(0, ROW_TILES // 8, dense, 0)

    def pick(c):
        def some(i, _):
            for u in range(16):
                n = i * 16 + u
                rows_tmp[pl.ds(n, 1), :] = block[pl.ds(rows_smem[c, 0, n], 1), :]
            return 0

        lax.fori_loop(0, NEW // 16, some, 0)
        return rows_tmp[...]

    first = []
    for j in ORDER + (0,):
        pick1[j] = pick(col_at(j, 1 - core)).astype(jnp.bfloat16)
        first.append(remote(pick1.at[j], pickr1.at[j], p1_send.at[j], p1_recv.at[j], sibling))
    second = []
    for copy, j in zip(first, ORDER + (0,)):
        mine = pick(col_at(j, core))
        copy.wait()
        value = mine + pickr1[j].astype(jnp.float32)
        if j == 0:
            out_ref[...] = value
        else:
            pick2[j] = value.astype(jnp.bfloat16)
            second.append(
                remote(pick2.at[j], pickr2.at[j], p2_send.at[j], p2_recv.at[j],
                       {"row": row, "col": col_at(j, core)})
            )
    for copy in second:
        copy.wait()
    total = out_ref[...]
    for j in range(1, 8):
        total = total + pickr2[j].astype(jnp.float32)
    square = jnp.sum(total * total, axis=1, keepdims=True)
    out_ref[...] = target[...] * total * lax.rsqrt(square + 1e-06)


def local(
    embed, degree, tile_row, tile_col, tile_count, tile_values, new_rows, new_bucket, bucket_norm
):
    smem = pl.BlockSpec(memory_space=pltpu.SMEM)
    vmem = pl.BlockSpec(memory_space=pltpu.VMEM)
    bf16, f32 = jnp.bfloat16, jnp.float32
    dma = pltpu.SemaphoreType.DMA
    return pl.pallas_call(
        kernel,
        name="propagate",
        out_shape=jax.ShapeDtypeStruct((NEW, TILE), f32),
        in_specs=[smem] * 2 + [vmem] * 6 + [pl.BlockSpec(memory_space=pl.ANY)],
        out_specs=vmem,
        scratch_shapes=[
            pltpu.VMEM((8, SLOTS), jnp.int32),
            pltpu.SMEM((8, SLOTS), jnp.int32),
            pltpu.VMEM((PIECE, TILE, TILE), f32),
            pltpu.VMEM((NEW, TILE), f32),
            pltpu.VMEM((SLOTS + 1, TILE, TILE), bf16),
            pltpu.VMEM((32, TILE, TILE), bf16),
            pltpu.VMEM((32, TILE, TILE), bf16),
            pltpu.VMEM((32, TILE, TILE), bf16),
            pltpu.VMEM((PAIRS + 1, TILE, TILE), f32),
            pltpu.VMEM((ROW_TILES * TILE, TILE), f32),
            pltpu.VMEM((2, CHUNKS, 8, CHUNK, TILE, TILE), bf16),
            pltpu.VMEM((2, CHUNKS, 8, CHUNK, TILE, TILE), bf16),
            pltpu.VMEM((2, CHUNKS, 8, CHUNK, TILE, TILE), bf16),
            pltpu.VMEM((2, CHUNKS, 8, CHUNK, TILE, TILE), bf16),
            pltpu.VMEM((2, CHUNKS, 4, CHUNK, TILE, TILE), bf16),
            pltpu.VMEM((2, CHUNKS, 4, CHUNK, TILE, TILE), bf16),
            pltpu.VMEM((CHUNKS, 4, CHUNK, TILE, TILE), f32),
            pltpu.VMEM((16, 1, NEW), jnp.int32),
            pltpu.SMEM((16, 1, NEW), jnp.int32),
            pltpu.VMEM((NEW, TILE), f32),
            pltpu.VMEM((8, NEW, TILE), bf16),
            pltpu.VMEM((8, NEW, TILE), bf16),
            pltpu.VMEM((8, NEW, TILE), bf16),
            pltpu.VMEM((8, NEW, TILE), bf16),
            dma, dma, dma,
            dma((HOPS, CHUNKS, 7)), dma((HOPS, CHUNKS, 7)), dma((2, CHUNKS)), dma((2, CHUNKS)),
            dma((2, CHUNKS, 4)), dma((2, CHUNKS, 4)), dma((2, CHUNKS, 4)), dma((2, CHUNKS, 4)), dma((16,)), dma((16,)),
            dma((8,)), dma((8,)), dma((8,)), dma((8,)),
        ],
        compiler_params=pltpu.CompilerParams(
            collective_id=0, has_side_effects=True, vmem_limit_bytes=56 << 20
        ),
    )(
        tile_count, bucket_norm, embed.reshape(PIECE, TILE, TILE), degree.reshape(PIECE, TILE),
        tile_row[0], tile_col[0], new_rows.reshape(1, NEW), new_bucket.reshape(NEW // TILE, TILE),
        tile_values[0, 0],
    )


def solution(mesh):
    in_specs = (
        P(("row", "col"), None),
        P(("row", "col")),
        P("row", "col", None),
        P("row", "col", None),
        P("row", "col"),
        P("row", "col", None, None, None),
        P(("row", "col")),
        P(("row", "col")),
        P(),
    )
    out_specs = P(("row", "col"), None)
    return jax.shard_map(local, mesh=mesh, in_specs=in_specs, out_specs=out_specs, check_vma=False)
```
